32 devices in a mesh: fsdp: 8 (over z, x), tp: 4 (over y, core).
Axes of the slice: x: 2, y: 2, z: 4, core: 2. Of those that a mesh axis runs over, the one named last changes fastest.
Arguments:
- tokens: bfloat16 [1024, 16, 768], P('tp', 'fsdp'), may hold values from -6 to 6
- cotangent: bfloat16 [1024, 16, 768], P('tp', 'fsdp'), may hold values from -6 to 6
- lengths: int32 [16], P('fsdp'), may hold values from 256 to 1024, as said below
- qkv_weight: bfloat16 [768, 576], P('tp', 'fsdp'), may hold values from -0.4375 to 0.4375
- out_weight: bfloat16 [768, 768], P('tp', 'fsdp'), may hold values from -3.5 to 3.5
- in_weight: bfloat16 [768, 768], P('tp', 'fsdp'), may hold values from -0.4375 to 0.4375
- down_weight: bfloat16 [3072, 192], P('tp', 'fsdp'), may hold values from -0.3125 to 0.3125
- gains: float32 [2, 768], replicated, may hold values from 0.5 to 1.5
- biases: float32 [2, 768], replicated, may hold values from -2 to 2
Outputs:
- output: bfloat16 [1024, 16, 768], P('tp', 'fsdp')
- d_input: float32 [1024, 16, 768], P('tp', 'fsdp')
- d_qkv_weight: float32 [768, 576], P('tp', 'fsdp')
- d_out_weight: float32 [768, 768], P('tp', 'fsdp')
- d_in_weight: float32 [768, 768], P('tp', 'fsdp')
- d_down_weight: float32 [3072, 192], P('tp', 'fsdp')
- d_gains: float32 [2, 768], replicated
- d_biases: float32 [2, 768], replicated
- rms: float32 [3], replicated
The draws below stay inside these ranges and needn't reach their ends.
Inputs may be any that keep to these rules, and one draw needn't show every extreme that they name: `lengths`: valid positions of each sequence slot, counted from its first position; every draw has a slot of exactly 1024 and one of exactly 256 valid positions.
All inputs are finite; a program needn't handle non-finite values.
Results may differ from the reference program's by a relative error of at most 0.02.
Values may be sent and summed in bfloat16 or wider, within the bound.
No kernel may reach another device: no remote copies, remote signals or barrier semaphores. Data moves between devices by JAX's collectives and lax.ppermute only.
A program may use at most 128 MiB of HBM per device.

```python
import jax
import jax.numpy as jnp
from jax import lax

D = 768
HD = 64
FF = 3072
GROUPS = 4
SLOT = 1024
SEQ_GRP = 2
D_G = 192
FF_G = 768
HPG = 3
SEQS = 16


def draw_lengths(key, part):
    drawn = jax.random.randint(key, (SEQS,), SLOT // 4, SLOT + 1, dtype=jnp.int32)
    slots = jnp.arange(SEQS, dtype=jnp.int32)
    drawn = jnp.where(slots == 0, SLOT, drawn)
    drawn = jnp.where(slots == SEQS - 1, SLOT // 4, drawn)
    return drawn.astype(jnp.int32)


def steps_of(stream_key, shape, shards, least, largest):
    def one(dim, blocks):
        steps = jax.random.uniform(jax.random.fold_in(jax.random.fold_in(stream_key, 6), dim), (blocks,), jnp.float32, least / len(shards), largest / len(shards))
        return jnp.repeat(jnp.exp(steps), shape[dim] // blocks).reshape((-1,) + (1,) * (len(shape) - dim - 1))

    loudness = one(*shards[0])
    for cut in shards[1:]:
        loudness = loudness * one(*cut)
    return loudness


def gaussian(own_key, dims, scale, most, pieces=(), kind=jnp.bfloat16):
    result = scale * jax.random.normal(own_key, dims, jnp.float32)
    if pieces:
        result = result * steps_of(own_key, dims, pieces, -0.22, 0.18)
    return jnp.clip(result, -most, most).astype(kind)


def setup_inputs(seed: int = 0) -> dict:
    keys = jax.random.split(jax.random.key(seed), 10)
    tokens = gaussian(keys[0], (SLOT, SEQS, D), 1.0, 6.0, ((0, 4), (1, 8)))
    cotangent = gaussian(keys[1], (SLOT, SEQS, D), 1.0, 6.0, ((0, 4), (1, 8)))
    lengths = draw_lengths(jax.random.fold_in(keys[9], 71), 0)
    qkv_weight = gaussian(keys[3], (D, 3 * D_G), D_G ** -0.5, 0.4375, ((0, 4), (1, 8)))
    out_weight = gaussian(keys[4], (D, D), 3 ** -0.5, 3.5, ((0, 4), (1, 8)))
    in_weight = gaussian(keys[5], (D, FF_G), D_G ** -0.5, 0.4375, ((0, 4), (1, 8)))
    down_weight = gaussian(keys[6], (FF, D_G), (FF_G // 2) ** -0.5, 0.3125, ((0, 4), (1, 8)))
    gains = jnp.clip(1.0 + 0.1 * jax.random.normal(keys[7], (2, D), jnp.float32), 0.5, 1.5)
    biases = gaussian(keys[8], (2, D), 0.3, 2.0, (), jnp.float32)
    return {"tokens": tokens, "cotangent": cotangent, "lengths": lengths, "qkv_weight": qkv_weight, "out_weight": out_weight, "in_weight": in_weight, "down_weight": down_weight, "gains": gains, "biases": biases}


@jax.custom_vjp
def low(v):
    return lax.optimization_barrier(v.astype(jnp.bfloat16)).astype(jnp.float32)

@jax.custom_vjp
def low_back(v):
    return v

def low_keep(v):
    return (low(v), None)

def low_pass(kept, grad):
    return (grad,)

def back_keep(v):
    return (v, None)

def back_low(kept, grad):
    return (low(grad),)
low.defvjp(low_keep, low_pass)
low_back.defvjp(back_keep, back_low)
highest = lax.Precision.HIGHEST
score_scale = 0.125
ln_epsilon = 1e-12
neg_fill = -1e+30

def norm_rows(summed, gain_row, bias_row):
    row_mean = lax.optimization_barrier(jnp.mean(summed, axis=-1, keepdims=True))
    centered = summed - row_mean
    variance = lax.optimization_barrier(jnp.mean(centered * centered, axis=-1, keepdims=True))
    return centered * lax.rsqrt(variance + ln_epsilon) * gain_row + bias_row

def layer_forward(tokens, qkv_weight, out_weight, in_weight, down_weight, gains, biases, valid_rows):
    positions = tokens.shape[0]
    sequences = tokens.shape[1]
    grouped = low_back(tokens).reshape(positions, sequences, GROUPS, D_G)
    projected = jnp.einsum('pngc,gcf->pngf', grouped, qkv_weight.reshape(GROUPS, D_G, 3 * D_G), precision=highest)
    projected = low_back(low(projected)).reshape(positions, sequences, GROUPS, 3, HPG, HD)
    query_heads = projected[:, :, :, 0]
    key_heads = projected[:, :, :, 1]
    value_heads = projected[:, :, :, 2]
    raw_scores = jnp.einsum('qnghd,knghd->nghqk', query_heads, key_heads, precision=highest) * score_scale
    raw_scores = low_back(raw_scores)
    key_valid = jnp.transpose(valid_rows)[:, None, None, None, :] > 0.5
    masked = jnp.where(key_valid, raw_scores, neg_fill)
    attn_probs = low_back(low(jax.nn.softmax(masked, axis=-1)))
    context = jnp.einsum('nghqk,knghd->qnghd', attn_probs, value_heads, precision=highest)
    context = low_back(low(context)).reshape(positions, sequences, GROUPS, D_G)
    partial_mix = jnp.einsum('pngc,gco->pngo', context, out_weight.reshape(GROUPS, D_G, D), precision=highest)
    attention_result_rows = low_back(lax.optimization_barrier(jnp.sum(low(partial_mix), axis=2)))
    first_normalized_rows = norm_rows(tokens + attention_result_rows, gains[0], biases[0])
    ffn_input = low_back(low(first_normalized_rows)).reshape(positions, sequences, GROUPS, D_G)
    pre_act = jnp.einsum('pngc,gcf->pngf', ffn_input, in_weight.reshape(GROUPS, D_G, FF_G), precision=highest)
    pre_act = low_back(pre_act)
    hidden = low_back(low(jax.nn.gelu(pre_act, approximate=False)))
    ffn_result = jnp.einsum('pngf,gfo->pngo', hidden, down_weight.reshape(GROUPS, FF_G, D_G), precision=highest)
    ffn_result = low_back(low(ffn_result)).reshape(positions, sequences, D)
    valid_cols = valid_rows[:, :, None]
    output = norm_rows(first_normalized_rows + ffn_result, gains[1], biases[1]) * valid_cols
    statistics = jnp.stack([jnp.sum(valid_cols * tokens * tokens), jnp.sum(valid_cols * attention_result_rows * attention_result_rows), jnp.sum(valid_cols * ffn_result * ffn_result), jnp.sum(valid_rows)])
    return (output, statistics)

def reference(tokens, cotangent, lengths, qkv_weight, out_weight, in_weight, down_weight, gains, biases):
    weights = (qkv_weight.astype(jnp.float32), out_weight.astype(jnp.float32), in_weight.astype(jnp.float32), down_weight.astype(jnp.float32))
    spots = jnp.arange(SLOT, dtype=jnp.int32)
    valid_all = (spots[:, None] < lengths[None, :].astype(jnp.int32)).astype(jnp.float32)
    span_count = SEQS // SEQ_GRP

    def span_step(running, span_index):
        first_seq = (span_index * SEQ_GRP).astype(jnp.int32)
        span_tokens = lax.dynamic_slice_in_dim(tokens, first_seq, SEQ_GRP, 1).astype(jnp.float32)
        span_grads = lax.dynamic_slice_in_dim(cotangent, first_seq, SEQ_GRP, 1).astype(jnp.float32)
        span_valid = lax.dynamic_slice_in_dim(valid_all, first_seq, SEQ_GRP, 1)

        def forward(token_in, w_qkv, w_out, w_in, w_down, gain_in, bias_in):
            return layer_forward(token_in, w_qkv, w_out, w_in, w_down, gain_in, bias_in, span_valid)
        output, pullback, statistics = jax.vjp(forward, span_tokens, weights[0], weights[1], weights[2], weights[3], gains, biases, has_aux=True)
        grads = pullback(span_grads)
        totals = tuple((old + new for old, new in zip(running[0], grads[1:])))
        return ((totals, running[1] + statistics), (output.astype(jnp.bfloat16), grads[0]))
    shapes = [matrix.shape for matrix in weights] + [gains.shape, biases.shape]
    init = (tuple((jnp.zeros(shape, jnp.float32) for shape in shapes)), jnp.zeros((4,), jnp.float32))
    (totals, stat_sums), (outputs, input_grads) = lax.scan(span_step, init, jnp.arange(span_count, dtype=jnp.int32))
    output = jnp.moveaxis(outputs, 0, 1).reshape(SLOT, SEQS, D)
    d_input = jnp.moveaxis(input_grads, 0, 1).reshape(SLOT, SEQS, D)
    rms = jnp.sqrt(stat_sums[:3] / (stat_sums[3] * D))
    return (output, d_input, totals[0], totals[1], totals[2], totals[3], totals[4], totals[5], rms)
```

```python
from functools import partial

import jax
import jax.numpy as jnp
from jax import lax
from jax.experimental import pallas as pl
from jax.experimental.pallas import tpu as pltpu
from jax.sharding import PartitionSpec as P

HD = 64
LANES = 128
SCALE = 0.125
EPS = 1e-12
NEG = -1e30
RSQRT2 = 0.7071067811865476
RSQRT2PI = 0.3989422804014327
F32 = jnp.float32
BF16 = jnp.bfloat16


def dot_nn(a, b):
    return lax.dot_general(a, b, (((1,), (0,)), ((), ())), preferred_element_type=F32)


def dot_nt(a, b):
    return lax.dot_general(a, b, (((1,), (1,)), ((), ())), preferred_element_type=F32)


def dot_tn(a, b):
    return lax.dot_general(a, b, (((0,), (0,)), ((), ())), preferred_element_type=F32)


def pack(value):
    half = value.shape[0] // 2
    tail = value[:, LANES:]
    return jnp.concatenate(
        [value[:, :LANES], jnp.concatenate([tail[:half], tail[half:]], axis=1)], axis=0
    )


def unpack(block):
    rows = block.shape[0] * 2 // 3
    tail = block[rows:]
    return jnp.concatenate(
        [block[:rows], jnp.concatenate([tail[:, :HD], tail[:, HD:]], axis=0)], axis=1
    )


def split_kernel(tok_ref, cot_ref, tok_out, cot_out, send_out):
    groups = send_out.shape[0]
    width = tok_ref.shape[2] // groups
    for n in range(tok_ref.shape[1]):
        rows = tok_ref[:, n, :]
        tok_out[n] = rows
        cot_out[n] = cot_ref[:, n, :]
        for g in range(groups):
            send_out[g, n] = pack(rows[:, g * width : (g + 1) * width])


def attend_kernel(len_ref, x_ref, w_ref, ctx_ref, lse_ref, proj, block):
    n = pl.program_id(0)
    length = len_ref[n]
    parts = x_ref.shape[0]
    width = w_ref.shape[1]
    heads = width // HD
    keys_all = parts * block
    x = jnp.concatenate([unpack(x_ref[i, 0]) for i in range(parts)], axis=0)
    proj[...] = dot_nt(x, w_ref[...]).astype(BF16)
    ctx_ref[...] = jnp.zeros_like(ctx_ref)
    lse_ref[...] = jnp.zeros_like(lse_ref)
    half = block // 2
    for count in range(1, parts + 1):
        span = count * block

        @pl.when((length > span - block) & (length <= span))
        def _():
            spot = lax.broadcasted_iota(jnp.int32, (block, block), 0) + (span - block)
            alive = spot < length
            for h in range(heads):
                keys = proj[0:span, width + h * HD : width + (h + 1) * HD]
                values_t = proj[0:span, 2 * width + h * HD : 2 * width + (h + 1) * HD].T
                for b in range(count):
                    query = proj[b * block : (b + 1) * block, h * HD : (h + 1) * HD] * SCALE
                    raw = dot_nt(keys, query.astype(BF16))
                    last = jnp.where(alive, raw[span - block :], NEG)
                    masked = jnp.concatenate([raw[: span - block], last], axis=0) if count > 1 else last
                    top = jnp.max(masked, axis=0, keepdims=True)
                    terms = jnp.exp(masked - top)
                    total = jnp.sum(terms, axis=0, keepdims=True)
                    mixed = dot_nn(values_t, terms.astype(BF16)) / total
                    mixed = mixed.T.astype(BF16)
                    if h < 2:
                        ctx_ref[b, 0, 0:block, h * HD : (h + 1) * HD] = mixed
                    else:
                        ctx_ref[b, 0, block:, 0:HD] = mixed[:half]
                        ctx_ref[b, 0, block:, HD:] = mixed[half:]
                    lse_ref[0, h : h + 1, b * block : (b + 1) * block] = top + jnp.log(total)


def attend_back_kernel(
    len_ref, x_ref, w_ref, g_ref, ctx_ref, lse_ref, back_ref, dw_ref, proj, dproj, grad, delta, dkv, dw, block
):
    n = pl.program_id(0)
    length = len_ref[n]
    parts = x_ref.shape[0]
    width = w_ref.shape[1]
    heads = width // HD
    x = jnp.concatenate([unpack(x_ref[i, 0]) for i in range(parts)], axis=0)
    proj[...] = dot_nt(x, w_ref[...]).astype(BF16)
    for i in range(parts):
        piece = unpack(g_ref[i, 0])
        grad[i * block : (i + 1) * block] = piece
        both = piece.astype(F32) * unpack(ctx_ref[i, 0]).astype(F32)
        both_t = both.T
        for h in range(heads):
            delta[h : h + 1, i * block : (i + 1) * block] = jnp.sum(
                both_t[h * HD : (h + 1) * HD], axis=0, keepdims=True
            )
    dproj[...] = jnp.zeros_like(dproj)
    for count in range(1, parts + 1):
        span = count * block

        @pl.when((length > span - block) & (length <= span))
        def _():
            spot = lax.broadcasted_iota(jnp.int32, (block, block), 0) + (span - block)
            alive = spot < length
            for h in range(heads):
                q_cols = slice(h * HD, (h + 1) * HD)
                k_cols = slice(width + h * HD, width + (h + 1) * HD)
                v_cols = slice(2 * width + h * HD, 2 * width + (h + 1) * HD)
                keys = proj[0:span, k_cols]
                keys_t = keys.T
                values = proj[0:span, v_cols]
                dk = jnp.zeros((span, HD), F32)
                dv = jnp.zeros((span, HD), F32)
                for b in range(count):
                    rows = slice(b * block, (b + 1) * block)
                    query = (proj[rows, q_cols] * SCALE).astype(BF16)
                    upstream = grad[rows, q_cols]
                    raw = dot_nt(keys, query)
                    last = jnp.where(alive, raw[span - block :], NEG)
                    masked = jnp.concatenate([raw[: span - block], last], axis=0) if count > 1 else last
                    probs = jnp.exp(masked - lse_ref[0, h : h + 1, rows])
                    dprobs = dot_nt(values, upstream)
                    dscores = (probs * (dprobs - delta[h : h + 1, rows])).astype(BF16)
                    dv = dv + dot_nn(probs.astype(BF16), upstream)
                    dk = dk + dot_nn(dscores, query)
                    dq_t = dot_nn(keys_t, dscores) * SCALE
                    dproj[rows, q_cols] = dq_t.T.astype(BF16)
                dproj[0:span, k_cols] = dk.astype(BF16)
                dproj[0:span, v_cols] = dv.astype(BF16)

    @pl.when(n == 0)
    def _():
        dw[...] = jnp.zeros_like(dw)

    dprojected = dproj[...]
    dw[...] += dot_tn(dprojected, x)
    back = dot_nn(dprojected, w_ref[...]).astype(BF16)
    for i in range(parts):
        back_ref[i, 0] = pack(back[i * block : (i + 1) * block])

    @pl.when(n == pl.num_programs(0) - 1)
    def _():
        dw_ref[...] = dw[...].astype(BF16)


def mean_of(value):
    return jnp.mean(value, axis=-1, keepdims=True)


def col_sum(value):
    return jnp.sum(value, axis=0, keepdims=True)


def gelu_pair(pre):
    upper = 0.5 * (1.0 + lax.erf(pre * RSQRT2))
    slope = upper + pre * (jnp.exp(-0.5 * pre * pre) * RSQRT2PI)
    return pre * upper, slope


def middle_kernel(
    len_ref, place_ref,
    tok_ref, cot_ref, ctx_ref, own_a, far_a, own_d, far_d, gain_ref, bias_ref,
    out_ref, mix_ref, send_ref, keep_a, send_a, keep_d, send_d, stat_ref,
    w_out, w_in, w_down, hid, slope, acc_a, acc_d, stats,
):
    n = pl.program_id(0)
    place = place_ref[0]
    chip = place // 2
    core = lax.rem(place, 2)
    groups = ctx_ref.shape[0]
    rows = tok_ref.shape[1]
    model = tok_ref.shape[2]
    width = model // groups

    @pl.when(n == 0)
    def _():
        for s in range(groups // 2):
            pair = lax.rem(chip + s, 2) * 2
            for wide, deep, g in ((own_a, own_d, pair + core), (far_a, far_d, pair + 1 - core)):
                both = wide[s]
                w_out[g] = both[:, :width]
                w_in[g] = both[:, width:]
                w_down[g] = deep[s]
        acc_a[...] = jnp.zeros_like(acc_a)
        acc_d[...] = jnp.zeros_like(acc_d)
        stats[...] = jnp.zeros_like(stats)

    gain0, gain1 = gain_ref[0:1, :], gain_ref[1:2, :]
    bias0, bias1 = bias_ref[0:1, :], bias_ref[1:2, :]
    spot = lax.broadcasted_iota(jnp.int32, (rows, 1), 0) + place * rows
    valid = (spot < len_ref[n]).astype(F32)
    tokens = tok_ref[0].astype(F32)
    contexts = [unpack(ctx_ref[g, 0]) for g in range(groups)]
    attention = dot_nt(contexts[0], w_out[0])
    for g in range(1, groups):
        attention = attention + dot_nt(contexts[g], w_out[g])
    mixed = tokens + attention
    centered = mixed - mean_of(mixed)
    inv0 = lax.rsqrt(mean_of(centered * centered) + EPS)
    xhat0 = centered * inv0
    first = xhat0 * gain0 + bias0
    ffn_in = first.astype(BF16)
    pieces = []
    for g in range(groups):
        cols = slice(g * width, (g + 1) * width)
        pre = dot_nt(ffn_in[:, cols], w_in[g])
        hidden, tilt = gelu_pair(pre)
        hidden = hidden.astype(BF16)
        hid[g] = hidden
        slope[g] = tilt
        pieces.append(dot_nt(hidden, w_down[g]))
    ffn = jnp.concatenate(pieces, axis=1).astype(BF16).astype(F32)
    second = first + ffn
    centered = second - mean_of(second)
    inv1 = lax.rsqrt(mean_of(centered * centered) + EPS)
    xhat1 = centered * inv1
    out_ref[0] = ((xhat1 * gain1 + bias1) * valid).astype(BF16)
    upstream = cot_ref[0].astype(F32) * valid
    scaled = upstream * gain1
    g_second = inv1 * (scaled - mean_of(scaled) - xhat1 * mean_of(scaled * xhat1))
    g_ffn = g_second.astype(BF16)
    pieces = []
    for g in range(groups):
        cols = slice(g * width, (g + 1) * width)
        g_hidden = dot_nn(g_ffn[:, cols], w_down[g]).astype(BF16).astype(F32)
        g_pre = (g_hidden * slope[g]).astype(BF16)
        acc_d[g] += dot_tn(g_ffn[:, cols], hid[g])
        acc_a[1, g] += dot_tn(g_pre, ffn_in[:, cols])
        pieces.append(dot_nn(g_pre, w_in[g]))
    g_input = jnp.concatenate(pieces, axis=1).astype(BF16).astype(F32)
    upper = g_second + g_input
    scaled = upper * gain0
    g_mix = inv0 * (scaled - mean_of(scaled) - xhat0 * mean_of(scaled * xhat0))
    mix_ref[0] = g_mix
    g_attn = g_mix.astype(BF16)
    for g in range(groups):
        acc_a[0, g] += dot_tn(g_attn, contexts[g])
        send_ref[g, 0] = pack(dot_nn(g_attn, w_out[g]).astype(BF16))
    stats[0:1] += col_sum(upper * xhat0)
    stats[1:2] += col_sum(upstream * xhat1)
    stats[2:3] += col_sum(upper)
    stats[3:4] += col_sum(upstream)
    stats[4:5] += col_sum(tokens * tokens * valid)
    stats[5:6] += col_sum(attention * attention * valid)
    stats[6:7] += col_sum(ffn * ffn * valid)
    stats[7:8] += jnp.broadcast_to(jnp.sum(valid, axis=0, keepdims=True), (1, model))

    @pl.when(n == pl.num_programs(0) - 1)
    def _():
        for s in range(groups // 2):
            pair = lax.rem(chip + s, 2) * 2
            for wide, deep, g in ((keep_a, keep_d, pair + core), (send_a, send_d, pair + 1 - core)):
                wide[s] = jnp.concatenate([acc_a[0, g], acc_a[1, g]], axis=1).astype(BF16)
                deep[s] = acc_d[g].astype(BF16)
        stat_ref[...] = stats[...]


def flip(value, axis, bit):
    size = lax.axis_size(axis)
    return lax.ppermute(value, axis, [(i, i ^ bit) for i in range(size)])


def halves(value):
    high = value.astype(BF16)
    return jnp.concatenate([high, (value - high.astype(F32)).astype(BF16)], axis=0)


def whole(value):
    rows = value.shape[-2] // 2
    value = value.astype(F32)
    return value[..., :rows, :] + value[..., rows:, :]


def gather_blocks(block, axis):
    size = lax.axis_size(axis)
    return lax.all_to_all(jnp.broadcast_to(block[None], (size,) + block.shape), axis, 0, 0)


def on_device(tokens, cotangent, lengths, qkv_weight, out_weight, in_weight, down_weight, gains, biases):
    groups = lax.axis_size("tp")
    shards = lax.axis_size("fsdp")
    place = lax.axis_index("tp").astype(jnp.int32).reshape(1)
    rows, sequences, model = tokens.shape
    width = model // groups
    hidden = in_weight.shape[1] * shards
    positions = rows * groups
    packed = rows * 3 // 2
    vmem = pl.BlockSpec(memory_space=pltpu.VMEM)
    smem = pl.BlockSpec(memory_space=pltpu.SMEM)

    def shape(dims, kind):
        return jax.ShapeDtypeStruct(dims, kind)

    qkv_all = gather_blocks(qkv_weight.T, "fsdp").reshape(3 * width, width)
    wide_rows, deep_rows = model // shards, width // shards
    wide = jnp.concatenate([out_weight.T, in_weight.T], axis=1)
    deep = down_weight.T.reshape(deep_rows, 2, 2 * width).swapaxes(0, 1).reshape(-1, 2 * width)

    tok_rows, cot_rows, grouped = pl.pallas_call(
        split_kernel,
        out_shape=(
            shape((sequences, rows, model), BF16),
            shape((sequences, rows, model), BF16),
            shape((groups, sequences, packed, LANES), BF16),
        ),
        in_specs=[vmem] * 2,
        out_specs=(vmem,) * 3,
        name="split",
    )(tokens, cotangent)
    grouped = lax.all_to_all(grouped, "tp", 0, 0)

    gathered = gather_blocks(jnp.concatenate([wide, deep], axis=0), "fsdp")
    wide_all = gathered[:, :wide_rows].reshape(model, 2 * width)
    deep_all = (
        gathered[:, wide_rows:].reshape(shards, 2, deep_rows, 2 * width).swapaxes(1, 2).reshape(width, hidden)
    )
    own_a = jnp.stack([wide_all, flip(wide_all, "tp", 2)])
    own_d = jnp.stack([deep_all, flip(deep_all, "tp", 2)])
    far_a = flip(own_a, "tp", 1)
    far_d = flip(own_d, "tp", 1)

    def chunk(n):
        return (0, n, 0, 0)

    chunk_spec = pl.BlockSpec((groups, 1, packed, LANES), chunk)
    whole_spec = pl.BlockSpec((3 * width, width), lambda n: (0, 0))
    lse_spec = pl.BlockSpec((1, 8, positions), lambda n: (n, 0, 0))
    context, lse = pl.pallas_call(
        partial(attend_kernel, block=rows),
        grid=(sequences,),
        out_shape=(
            shape((groups, sequences, packed, LANES), BF16),
            shape((sequences, 8, positions), F32),
        ),
        in_specs=[smem, chunk_spec, whole_spec],
        out_specs=(chunk_spec, lse_spec),
        scratch_shapes=[pltpu.VMEM((positions, 3 * width), BF16)],
        name="attend",
    )(lengths, grouped, qkv_all)
    mine = lax.all_to_all(context, "tp", 0, 0)

    row_spec = pl.BlockSpec((1, rows, model), lambda n: (n, 0, 0))

    def fixed(*dims):
        return pl.BlockSpec(dims, lambda n: (0,) * len(dims))

    pairs = groups // 2
    wide_spec = fixed(pairs, model, 2 * width)
    deep_spec = fixed(pairs, width, hidden)
    out_rows, g_mix, g_context, keep_a, send_a, keep_d, send_d, stats = pl.pallas_call(
        middle_kernel,
        grid=(sequences,),
        out_shape=(
            shape((sequences, rows, model), BF16),
            shape((sequences, rows, model), F32),
            shape((groups, sequences, packed, LANES), BF16),
            shape((pairs, model, 2 * width), BF16),
            shape((pairs, model, 2 * width), BF16),
            shape((pairs, width, hidden), BF16),
            shape((pairs, width, hidden), BF16),
            shape((8, model), F32),
        ),
        in_specs=[
            smem, smem, row_spec, row_spec, chunk_spec,
            wide_spec, wide_spec, deep_spec, deep_spec, fixed(2, model), fixed(2, model),
        ],
        out_specs=(
            row_spec, row_spec, chunk_spec, wide_spec, wide_spec, deep_spec, deep_spec, fixed(8, model),
        ),
        scratch_shapes=[
            pltpu.VMEM((groups, model, width), BF16),
            pltpu.VMEM((groups, hidden, width), BF16),
            pltpu.VMEM((groups, width, hidden), BF16),
            pltpu.VMEM((groups, rows, hidden), BF16),
            pltpu.VMEM((groups, rows, hidden), F32),
            pltpu.VMEM((2, groups, model, width), F32),
            pltpu.VMEM((groups, width, hidden), F32),
            pltpu.VMEM((8, model), F32),
        ],
        name="middle",
    )(lengths, place, tok_rows, cot_rows, mine, own_a, far_a, own_d, far_d, gains, biases)
    g_grouped = lax.all_to_all(g_context, "tp", 0, 0)

    sum_a = (keep_a.astype(F32) + flip(send_a, "tp", 1).astype(F32)).astype(BF16)
    sum_d = (keep_d.astype(F32) + flip(send_d, "tp", 1).astype(F32)).astype(BF16)
    stats = stats + whole(flip(halves(stats), "tp", 1))
    sum_a = (sum_a[0].astype(F32) + flip(sum_a[1], "tp", 2).astype(F32)).astype(BF16)
    sum_d = (sum_d[0].astype(F32) + flip(sum_d[1], "tp", 2).astype(F32)).astype(BF16)
    stats = stats + whole(flip(halves(stats), "tp", 2))
    blocks = jnp.concatenate(
        [
            sum_a.reshape(shards, wide_rows, 2 * width),
            sum_d.reshape(shards, deep_rows, 2, 2 * width).swapaxes(1, 2).reshape(shards, -1, 2 * width),
            jnp.broadcast_to(halves(stats).reshape(1, -1, 2 * width), (shards, 32, 2 * width)),
        ],
        axis=1,
    )
    blocks = lax.all_to_all(blocks, "fsdp", 0, 0).astype(F32)
    edge = wide_rows + 2 * deep_rows
    grads = jnp.sum(blocks[:, :edge], axis=0)
    totals = jnp.sum(whole(blocks[:, edge:].reshape(shards, 16, model)), axis=0)
    d_out = grads[:wide_rows, :width].T
    d_in = grads[:wide_rows, width:].T
    d_down = grads[wide_rows:].reshape(2, deep_rows, 2 * width).swapaxes(0, 1).reshape(deep_rows, hidden).T
    rms = jnp.sqrt(jnp.sum(totals[4:7], axis=1) / (totals[7, 0] * model))

    back, d_qkv = pl.pallas_call(
        partial(attend_back_kernel, block=rows),
        grid=(sequences,),
        out_shape=(
            shape((groups, sequences, packed, LANES), BF16),
            shape((3 * width, width), BF16),
        ),
        in_specs=[smem, chunk_spec, whole_spec, chunk_spec, chunk_spec, lse_spec],
        out_specs=(chunk_spec, whole_spec),
        scratch_shapes=[
            pltpu.VMEM((positions, 3 * width), BF16),
            pltpu.VMEM((positions, 3 * width), BF16),
            pltpu.VMEM((positions, width), BF16),
            pltpu.VMEM((8, positions), F32),
            pltpu.VMEM((8, LANES), F32),
            pltpu.VMEM((3 * width, width), F32),
        ],
        name="attend_back",
    )(lengths, grouped, qkv_all, g_grouped, context, lse)
    back = lax.all_to_all(back, "tp", 0, 0)
    d_qkv = lax.all_to_all(d_qkv.reshape(shards, -1, width), "fsdp", 0, 0)
    d_qkv = jnp.sum(d_qkv.astype(F32), axis=0).T

    def join_kernel(out_ref, mix_ref, back_ref, out_all, in_all):
        for n in range(sequences):
            pulled = jnp.concatenate([unpack(back_ref[g, n]) for g in range(groups)], axis=1)
            in_all[:, n, :] = mix_ref[n] + pulled.astype(F32)
            out_all[:, n, :] = out_ref[n]

    output, d_input = pl.pallas_call(
        join_kernel,
        out_shape=(shape(tokens.shape, BF16), shape(tokens.shape, F32)),
        in_specs=[vmem] * 3,
        out_specs=(vmem,) * 2,
        name="join",
    )(out_rows, g_mix, back)
    return (output, d_input, d_qkv, d_out, d_in, d_down, totals[0:2], totals[2:4], rms)


def solution(mesh):
    in_specs = (
        P("tp", "fsdp", None),
        P("tp", "fsdp", None),
        P("fsdp"),
        P("tp", "fsdp"),
        P("tp", "fsdp"),
        P("tp", "fsdp"),
        P("tp", "fsdp"),
        P(),
        P(),
    )
    out_specs = (
        P("tp", "fsdp", None),
        P("tp", "fsdp", None),
        P("tp", "fsdp"),
        P("tp", "fsdp"),
        P("tp", "fsdp"),
        P("tp", "fsdp"),
        P(),
        P(),
        P(),
    )
    return jax.shard_map(
        on_device, mesh=mesh, in_specs=in_specs, out_specs=out_specs, check_vma=False
    )
```

```python
from functools import partial

import jax
import jax.numpy as jnp
from jax import lax
from jax.experimental import pallas as pl
from jax.experimental.pallas import tpu as pltpu
from jax.sharding import PartitionSpec as P


HD = 64
LANES = 128
SCALE = 0.125
EPS = 1e-12
NEG = -1e30
RSQRT2 = 0.7071067811865476
RSQRT2PI = 0.3989422804014327
F32 = jnp.float32
BF16 = jnp.bfloat16


def dot_nn(a, b):
    return lax.dot_general(a, b, (((1,), (0,)), ((), ())), preferred_element_type=F32)


def dot_nt(a, b):
    return lax.dot_general(a, b, (((1,), (1,)), ((), ())), preferred_element_type=F32)


def dot_tn(a, b):
    return lax.dot_general(a, b, (((0,), (0,)), ((), ())), preferred_element_type=F32)


def pack(value):
    half = value.shape[0] // 2
    tail = value[:, LANES:]
    return jnp.concatenate(
        [value[:, :LANES], jnp.concatenate([tail[:half], tail[half:]], axis=1)], axis=0
    )


def unpack(block):
    rows = block.shape[0] * 2 // 3
    tail = block[rows:]
    return jnp.concatenate(
        [block[:rows], jnp.concatenate([tail[:, :HD], tail[:, HD:]], axis=0)], axis=1
    )


def split_kernel(place_ref, tok_ref, tok_out, *rest):
    sends, held = rest[:-1], rest[-1]
    groups = len(sends)
    width = tok_ref.shape[2] // groups
    for n in range(tok_ref.shape[1]):
        rows = tok_ref[:, n, :]
        tok_out[n] = rows
        for g in range(groups):
            held[g, n] = pack(rows[:, g * width : (g + 1) * width])
    for s in range(groups):
        sends[s][...] = held[place_ref[0] ^ s]


def part_kernel(in_ref, out_ref):
    for n in range(in_ref.shape[1]):
        out_ref[n] = in_ref[:, n, :]


def merge_kernel(in_ref, out_ref):
    for n in range(in_ref.shape[0]):
        out_ref[:, n, :] = in_ref[n]


def join_kernel(place_ref, mix_ref, *rest):
    backs, out_ref, held = rest[:-2], rest[-2], rest[-1]
    groups = len(backs)
    for s in range(groups):
        held[place_ref[0] ^ s] = backs[s][...]
    for n in range(mix_ref.shape[0]):
        pulled = jnp.concatenate([unpack(held[g, n]) for g in range(groups)], axis=1)
        out_ref[:, n, :] = mix_ref[n] + pulled.astype(F32)


def attend_kernel(len_ref, place_ref, *rest, block, parts):
    chunk_refs, (w_ref, *sends), (lse_ref, tokens, proj, held) = rest[:parts], rest[parts : 2 * parts + 1], rest[2 * parts + 1 :]
    length = len_ref[pl.program_id(0)]
    width = w_ref.shape[1]
    heads = width // HD
    for s in range(parts):
        start = pl.multiple_of((place_ref[0] ^ s) * block, block)
        tokens[pl.ds(start, block)] = unpack(chunk_refs[s][0])
    proj[...] = dot_nt(tokens[...], w_ref[...]).astype(BF16)
    held[...] = jnp.zeros_like(held)
    lse_ref[...] = jnp.zeros_like(lse_ref)
    half = block // 2
    for count in range(1, parts + 1):
        span = count * block

        @pl.when((length > span - block) & (length <= span))
        def _():
            spot = lax.broadcasted_iota(jnp.int32, (block, block), 0) + (span - block)
            alive = spot < length
            for h in range(heads):
                keys = proj[0:span, width + h * HD : width + (h + 1) * HD]
                values_t = proj[0:span, 2 * width + h * HD : 2 * width + (h + 1) * HD].T
                for b in range(count):
                    query = proj[b * block : (b + 1) * block, h * HD : (h + 1) * HD] * SCALE
                    raw = dot_nt(keys, query.astype(BF16))
                    last = jnp.where(alive, raw[span - block :], NEG)
                    masked = jnp.concatenate([raw[: span - block], last], axis=0) if count > 1 else last
                    top = jnp.max(masked, axis=0, keepdims=True)
                    terms = jnp.exp(masked - top)
                    total = jnp.sum(terms, axis=0, keepdims=True)
                    mixed = dot_nn(values_t, terms.astype(BF16)) / total
                    mixed = mixed.T.astype(BF16)
                    if h < 2:
                        held[b, 0:block, h * HD : (h + 1) * HD] = mixed
                    else:
                        held[b, block:, 0:HD] = mixed[:half]
                        held[b, block:, HD:] = mixed[half:]
                    lse_ref[0, h : h + 1, b * block : (b + 1) * block] = top + jnp.log(total)

    for s in range(parts):
        sends[s][0] = held[place_ref[0] ^ s]


def attend_back_kernel(len_ref, place_ref, *rest, block, parts):
    chunk_refs, g_refs, ctx_refs = rest[:parts], rest[parts : 2 * parts], rest[2 * parts : 3 * parts]
    w_ref, lse_ref = rest[3 * parts : 3 * parts + 2]
    sends = rest[3 * parts + 2 : 4 * parts + 2]
    dw_ref, tokens, proj, dproj, grad, mixed, delta, dw, held = rest[4 * parts + 2 :]
    n = pl.program_id(0)
    length = len_ref[n]
    width = w_ref.shape[1]
    heads = width // HD
    for s in range(parts):
        start = pl.multiple_of((place_ref[0] ^ s) * block, block)
        tokens[pl.ds(start, block)] = unpack(chunk_refs[s][0])
        grad[pl.ds(start, block)] = unpack(g_refs[s][0])
        mixed[pl.ds(start, block)] = unpack(ctx_refs[s][0])
    proj[...] = dot_nt(tokens[...], w_ref[...]).astype(BF16)
    for i in range(parts):
        rows = slice(i * block, (i + 1) * block)
        both_t = (grad[rows].astype(F32) * mixed[rows].astype(F32)).T
        for h in range(heads):
            delta[h : h + 1, rows] = jnp.sum(both_t[h * HD : (h + 1) * HD], axis=0, keepdims=True)
    dproj[...] = jnp.zeros_like(dproj)
    for count in range(1, parts + 1):
        span = count * block

        @pl.when((length > span - block) & (length <= span))
        def _():
            spot = lax.broadcasted_iota(jnp.int32, (block, block), 0) + (span - block)
            alive = spot < length
            for h in range(heads):
                q_cols = slice(h * HD, (h + 1) * HD)
                k_cols = slice(width + h * HD, width + (h + 1) * HD)
                v_cols = slice(2 * width + h * HD, 2 * width + (h + 1) * HD)
                keys = proj[0:span, k_cols]
                keys_t = keys.T
                values = proj[0:span, v_cols]
                dk = jnp.zeros((span, HD), F32)
                dv = jnp.zeros((span, HD), F32)
                for b in range(count):
                    rows = slice(b * block, (b + 1) * block)
                    query = (proj[rows, q_cols] * SCALE).astype(BF16)
                    upstream = grad[rows, q_cols]
                    raw = dot_nt(keys, query)
                    last = jnp.where(alive, raw[span - block :], NEG)
                    masked = jnp.concatenate([raw[: span - block], last], axis=0) if count > 1 else last
                    probs = jnp.exp(masked - lse_ref[0, h : h + 1, rows])
                    dprobs = dot_nt(values, upstream)
                    dscores = (probs * (dprobs - delta[h : h + 1, rows])).astype(BF16)
                    dv = dv + dot_nn(probs.astype(BF16), upstream)
                    dk = dk + dot_nn(dscores, query)
                    dq_t = dot_nn(keys_t, dscores) * SCALE
                    dproj[rows, q_cols] = dq_t.T.astype(BF16)
                dproj[0:span, k_cols] = dk.astype(BF16)
                dproj[0:span, v_cols] = dv.astype(BF16)

    @pl.when(n == 0)
    def _():
        dw[...] = jnp.zeros_like(dw)

    dprojected = dproj[...]
    dw[...] += dot_tn(dprojected, tokens[...])
    back = dot_nn(dprojected, w_ref[...]).astype(BF16)
    for i in range(parts):
        held[i] = pack(back[i * block : (i + 1) * block])
    for s in range(parts):
        sends[s][0] = held[place_ref[0] ^ s]

    @pl.when(n == pl.num_programs(0) - 1)
    def _():
        dw_ref[...] = dw[...].astype(BF16)


def mean_of(value):
    return jnp.mean(value, axis=-1, keepdims=True)


def col_sum(value):
    return jnp.sum(value, axis=0, keepdims=True)


def gelu_pair(pre):
    upper = 0.5 * (1.0 + lax.erf(pre * RSQRT2))
    slope = upper + pre * (jnp.exp(-0.5 * pre * pre) * RSQRT2PI)
    return pre * upper, slope


def middle_kernel(len_ref, place_ref, *rest, groups):
    ctx_refs, rest = rest[:groups], rest[groups:]
    tok_ref, cot_ref, own_a, far_a, own_d, far_d, gain_ref, bias_ref, out_ref, mix_ref = rest[:10]
    sends, rest = rest[10 : 10 + groups], rest[10 + groups :]
    keep_a, send_a, keep_d, send_d, stat_ref, w_out, w_in, w_down, hid, slope, acc_a, acc_d, stats = rest
    n = pl.program_id(0)
    place = place_ref[0]
    chip = place // 2
    core = lax.rem(place, 2)
    rows = tok_ref.shape[1]
    model = tok_ref.shape[2]
    width = model // groups

    @pl.when(n == 0)
    def _():
        for s in range(groups // 2):
            pair = lax.rem(chip + s, 2) * 2
            for wide, deep, g in ((own_a, own_d, pair + core), (far_a, far_d, pair + 1 - core)):
                both = wide[s]
                w_out[g] = both[:, :width]
                w_in[g] = both[:, width:]
                w_down[g] = deep[s]
        acc_a[...] = jnp.zeros_like(acc_a)
        acc_d[...] = jnp.zeros_like(acc_d)
        stats[...] = jnp.zeros_like(stats)

    gain0, gain1 = gain_ref[0:1, :], gain_ref[1:2, :]
    bias0, bias1 = bias_ref[0:1, :], bias_ref[1:2, :]
    spot = lax.broadcasted_iota(jnp.int32, (rows, 1), 0) + place * rows
    valid = (spot < len_ref[n]).astype(F32)
    tokens = tok_ref[0].astype(F32)
    contexts = [unpack(ctx_refs[s][0]) for s in range(groups)]
    attention = dot_nt(contexts[0], w_out[place])
    for s in range(1, groups):
        attention = attention + dot_nt(contexts[s], w_out[place ^ s])
    mixed = tokens + attention
    centered = mixed - mean_of(mixed)
    inv0 = lax.rsqrt(mean_of(centered * centered) + EPS)
    xhat0 = centered * inv0
    first = xhat0 * gain0 + bias0
    ffn_in = first.astype(BF16)
    pieces = []
    for g in range(groups):
        cols = slice(g * width, (g + 1) * width)
        pre = dot_nt(ffn_in[:, cols], w_in[g])
        hidden, tilt = gelu_pair(pre)
        hidden = hidden.astype(BF16)
        hid[g] = hidden
        slope[g] = tilt
        pieces.append(dot_nt(hidden, w_down[g]))
    ffn = jnp.concatenate(pieces, axis=1).astype(BF16).astype(F32)
    second = first + ffn
    centered = second - mean_of(second)
    inv1 = lax.rsqrt(mean_of(centered * centered) + EPS)
    xhat1 = centered * inv1
    out_ref[0] = ((xhat1 * gain1 + bias1) * valid).astype(BF16)
    upstream = cot_ref[0].astype(F32) * valid
    scaled = upstream * gain1
    g_second = inv1 * (scaled - mean_of(scaled) - xhat1 * mean_of(scaled * xhat1))
    g_ffn = g_second.astype(BF16)
    pieces = []
    for g in range(groups):
        cols = slice(g * width, (g + 1) * width)
        g_hidden = dot_nn(g_ffn[:, cols], w_down[g]).astype(BF16).astype(F32)
        g_pre = (g_hidden * slope[g]).astype(BF16)
        acc_d[g] += dot_tn(g_ffn[:, cols], hid[g])
        acc_a[1, g] += dot_tn(g_pre, ffn_in[:, cols])
        pieces.append(dot_nn(g_pre, w_in[g]))
    g_input = jnp.concatenate(pieces, axis=1).astype(BF16).astype(F32)
    upper = g_second + g_input
    scaled = upper * gain0
    g_mix = inv0 * (scaled - mean_of(scaled) - xhat0 * mean_of(scaled * xhat0))
    mix_ref[0] = g_mix
    g_attn = g_mix.astype(BF16)
    for s in range(groups):
        acc_a[0, place ^ s] += dot_tn(g_attn, contexts[s])
        sends[s][0] = pack(dot_nn(g_attn, w_out[place ^ s]).astype(BF16))
    stats[0:1] += col_sum(upper * xhat0)
    stats[1:2] += col_sum(upstream * xhat1)
    stats[2:3] += col_sum(upper)
    stats[3:4] += col_sum(upstream)
    stats[4:5] += col_sum(tokens * tokens * valid)
    stats[5:6] += col_sum(attention * attention * valid)
    stats[6:7] += col_sum(ffn * ffn * valid)
    stats[7:8] += jnp.broadcast_to(jnp.sum(valid, axis=0, keepdims=True), (1, model))

    @pl.when(n == pl.num_programs(0) - 1)
    def _():
        for s in range(groups // 2):
            pair = lax.rem(chip + s, 2) * 2
            for wide, deep, g in ((keep_a, keep_d, pair + core), (send_a, send_d, pair + 1 - core)):
                wide[s] = jnp.concatenate([acc_a[0, g], acc_a[1, g]], axis=1).astype(BF16)
                deep[s] = acc_d[g].astype(BF16)
        stat_ref[...] = stats[...]


def halves(value):
    high = value.astype(BF16)
    return jnp.concatenate([high, (value - high.astype(F32)).astype(BF16)], axis=0)


def whole(value):
    rows = value.shape[-2] // 2
    value = value.astype(F32)
    return value[..., :rows, :] + value[..., rows:, :]


def exchange(value, axis):
    return lax.all_to_all(value, axis, 0, 0)


def flip(value, axis, bit):
    size = lax.axis_size(axis)
    return lax.ppermute(value, axis, [(i, i ^ bit) for i in range(size)])


def tp_exchange(chunks):
    order = sorted(range(1, len(chunks)), reverse=True)
    moved = {s: flip(chunks[s], "tp", s) for s in order}
    return [chunks[0]] + [moved[s] for s in range(1, len(chunks))]


def gather_blocks(block, axis):
    size = lax.axis_size(axis)
    return exchange(jnp.broadcast_to(block[None], (size,) + block.shape), axis)


def far_groups(size):
    return [[i for i in range(size) if i % 2 == bit] for bit in range(2)]


def far_exchange(value):
    groups = far_groups(lax.axis_size("fsdp"))
    return lax.all_to_all(value, "fsdp", 0, 0, axis_index_groups=groups)


def add_low(*values):
    total = values[0].astype(F32)
    for value in values[1:]:
        total = total + value.astype(F32)
    return total.astype(BF16)


def on_device(tokens, cotangent, lengths, qkv_weight, out_weight, in_weight, down_weight, gains, biases):
    groups = lax.axis_size("tp")
    shards = lax.axis_size("fsdp")
    place = lax.axis_index("tp").astype(jnp.int32).reshape(1)
    rows, sequences, model = tokens.shape
    width = model // groups
    hidden = in_weight.shape[1] * shards
    positions = rows * groups
    packed = rows * 3 // 2
    pairs = groups // 2
    vmem = pl.BlockSpec(memory_space=pltpu.VMEM)
    smem = pl.BlockSpec(memory_space=pltpu.SMEM)

    def shape(dims, kind):
        return jax.ShapeDtypeStruct(dims, kind)

    def call(kernel, **options):
        def run(*operands):
            return pl.pallas_call(kernel, **options)(*operands)

        return run

    qkv_all = gather_blocks(qkv_weight.T, "fsdp").reshape(3 * width, width)
    wide_rows, deep_rows = model // shards, width // shards
    wide = jnp.concatenate([out_weight.T, in_weight.T], axis=1)
    deep = down_weight.T.reshape(deep_rows, 2, 2 * width).swapaxes(0, 1).reshape(-1, 2 * width)

    side = lax.rem(lax.axis_index("fsdp"), 2) == 0
    chunk_shape = shape((sequences, packed, LANES), BF16)
    by_sequence = shape((sequences, rows, model), BF16)
    held = pltpu.VMEM((groups, sequences, packed, LANES), BF16)
    tok_rows, *grouped = call(
        split_kernel,
        out_shape=(by_sequence,) + (chunk_shape,) * groups,
        in_specs=[smem, vmem],
        out_specs=(vmem,) * (1 + groups),
        scratch_shapes=[held],
    )(place, tokens)
    cot_rows = call(part_kernel, out_shape=by_sequence, in_specs=[vmem], out_specs=vmem)(cotangent)
    grouped = tp_exchange(grouped)

    block = jnp.concatenate([wide, deep], axis=0)
    near = far_exchange(jnp.broadcast_to(block[None], (shards // 2,) + block.shape))
    other = flip(near, "fsdp", 1)
    blocks = jnp.stack([jnp.where(side, near, other), jnp.where(side, other, near)], axis=1)
    wide_all = blocks[:, :, :wide_rows].reshape(model, 2 * width)
    deep_all = (
        blocks[:, :, wide_rows:].reshape(shards, 2, deep_rows, 2 * width).swapaxes(1, 2).reshape(width, hidden)
    )
    own_a = jnp.stack([wide_all, flip(wide_all, "tp", 2)])
    own_d = jnp.stack([deep_all, flip(deep_all, "tp", 2)])
    far_a = flip(own_a, "tp", 1)
    far_d = flip(own_d, "tp", 1)

    def fixed(*dims):
        return pl.BlockSpec(dims, lambda n: (0,) * len(dims))

    chunk_spec = pl.BlockSpec((1, packed, LANES), lambda n: (n, 0, 0))
    chunk_specs = (chunk_spec,) * groups
    whole_spec = fixed(3 * width, width)
    lse_spec = pl.BlockSpec((1, 8, positions), lambda n: (n, 0, 0))
    *context, lse = call(
        partial(attend_kernel, block=rows, parts=groups),
        grid=(sequences,),
        out_shape=(chunk_shape,) * groups + (shape((sequences, 8, positions), F32),),
        in_specs=[smem, smem, *chunk_specs, whole_spec],
        out_specs=(*chunk_specs, lse_spec),
        scratch_shapes=[
            pltpu.VMEM((positions, width), BF16),
            pltpu.VMEM((positions, 3 * width), BF16),
            pltpu.VMEM((groups, packed, LANES), BF16),
        ],
    )(lengths, place, *grouped, qkv_all)
    mine = tp_exchange(context)

    row_spec = pl.BlockSpec((1, rows, model), lambda n: (n, 0, 0))
    wide_spec = fixed(pairs, model, 2 * width)
    deep_spec = fixed(pairs, width, hidden)
    out_rows, g_mix, *rest = call(
        partial(middle_kernel, groups=groups),
        grid=(sequences,),
        out_shape=(
            by_sequence,
            shape((sequences, rows, model), F32),
            *(chunk_shape,) * groups,
            shape((pairs, model, 2 * width), BF16),
            shape((pairs, model, 2 * width), BF16),
            shape((pairs, width, hidden), BF16),
            shape((pairs, width, hidden), BF16),
            shape((8, model), F32),
        ),
        in_specs=[
            smem, smem, *chunk_specs, row_spec, row_spec,
            wide_spec, wide_spec, deep_spec, deep_spec, fixed(2, model), fixed(2, model),
        ],
        out_specs=(
            row_spec, row_spec, *chunk_specs, wide_spec, wide_spec, deep_spec, deep_spec, fixed(8, model),
        ),
        scratch_shapes=[
            pltpu.VMEM((groups, model, width), BF16),
            pltpu.VMEM((groups, hidden, width), BF16),
            pltpu.VMEM((groups, width, hidden), BF16),
            pltpu.VMEM((groups, rows, hidden), BF16),
            pltpu.VMEM((groups, rows, hidden), F32),
            pltpu.VMEM((2, groups, model, width), F32),
            pltpu.VMEM((groups, width, hidden), F32),
            pltpu.VMEM((8, model), F32),
        ],
    )(lengths, place, *mine, tok_rows, cot_rows, own_a, far_a, own_d, far_d, gains, biases)
    g_grouped = tp_exchange(rest[:groups])
    keep_a, send_a, keep_d, send_d, stats = rest[groups:]
    output = call(merge_kernel, out_shape=shape(tokens.shape, BF16), in_specs=[vmem], out_specs=vmem)(out_rows)

    sum_a = add_low(keep_a, flip(send_a, "tp", 1))
    sum_d = add_low(keep_d, flip(send_d, "tp", 1))
    stats = stats + whole(flip(halves(stats), "tp", 1))
    sum_a = add_low(sum_a[0], flip(sum_a[1], "tp", 2))
    sum_d = add_low(sum_d[0], flip(sum_d[1], "tp", 2))
    stats = stats + whole(flip(halves(stats), "tp", 2))

    *back, d_qkv = call(
        partial(attend_back_kernel, block=rows, parts=groups),
        grid=(sequences,),
        out_shape=(chunk_shape,) * groups + (shape((3 * width, width), BF16),),
        in_specs=[smem, smem, *chunk_specs * 3, whole_spec, lse_spec],
        out_specs=(*chunk_specs, whole_spec),
        scratch_shapes=[
            pltpu.VMEM((positions, width), BF16),
            pltpu.VMEM((positions, 3 * width), BF16),
            pltpu.VMEM((positions, 3 * width), BF16),
            pltpu.VMEM((positions, width), BF16),
            pltpu.VMEM((positions, width), BF16),
            pltpu.VMEM((8, positions), F32),
            pltpu.VMEM((3 * width, width), F32),
            pltpu.VMEM((groups, packed, LANES), BF16),
        ],
    )(lengths, place, *grouped, *g_grouped, *context, qkv_all, lse)
    back = tp_exchange(back)

    small = d_qkv.reshape(shards, -1, width)
    split = small.shape[1] % 2 == 0
    if split:
        small = jnp.concatenate([small[:, : small.shape[1] // 2], small[:, small.shape[1] // 2 :]], axis=2)
    else:
        small = jnp.pad(small, ((0, 0), (0, 0), (0, width)))
    pieces = [
        sum_a.reshape(shards, wide_rows, 2 * width),
        sum_d.reshape(shards, deep_rows, hidden)[:, :, : 2 * width],
        sum_d.reshape(shards, deep_rows, hidden)[:, :, 2 * width :],
        small,
        jnp.broadcast_to(halves(stats).reshape(1, -1, 2 * width), (shards, 32, 2 * width)),
    ]
    edges = [0]
    for piece in pieces:
        edges.append(edges[-1] + piece.shape[1])
    blocks = jnp.concatenate(pieces, axis=1)
    blocks = blocks.reshape((shards // 2, 2) + blocks.shape[1:])
    sent = flip(jnp.where(side, blocks[:, 1], blocks[:, 0]), "fsdp", 1)
    kept = jnp.where(side, blocks[:, 0], blocks[:, 1])
    mass, low = kept[:, : edges[4]], kept[:, edges[4] :].reshape(shards // 2, 16, model)
    mass = add_low(mass, sent[:, : edges[4]])
    low = whole(low) + whole(sent[:, edges[4] :].reshape(shards // 2, 16, model))
    low = jnp.concatenate([low.astype(BF16), (low - low.astype(BF16).astype(F32)).astype(BF16)], axis=1)
    blocks = jnp.concatenate([mass, low.reshape(shards // 2, 32, 2 * width)], axis=1)
    blocks = far_exchange(blocks).astype(F32)
    grads = jnp.sum(blocks[:, : edges[4]], axis=0)
    totals = jnp.sum(whole(blocks[:, edges[4] :].reshape(shards // 2, 16, model)), axis=0)
    d_wide, d_left, d_right, small = (grads[edges[i] : edges[i + 1]] for i in range(4))
    d_deep = jnp.concatenate([d_left, d_right], axis=1)
    d_qkv = jnp.concatenate([small[:, :width], small[:, width:]], axis=0) if split else small[:, :width]
    d_qkv = d_qkv.T
    rms = jnp.sqrt(jnp.sum(totals[4:7], axis=1) / (totals[7, 0] * model))

    d_input = call(
        join_kernel,
        out_shape=shape(tokens.shape, F32),
        in_specs=[smem] + [vmem] * (1 + groups),
        out_specs=vmem,
        scratch_shapes=[held],
    )(place, g_mix, *back)
    return (
        output, d_input, d_qkv, d_wide[:, :width].T, d_wide[:, width:].T, d_deep.T, totals[0:2], totals[2:4], rms,
    )


def solution(mesh):
    in_specs = (
        P("tp", "fsdp", None),
        P("tp", "fsdp", None),
        P("fsdp"),
        P("tp", "fsdp"),
        P("tp", "fsdp"),
        P("tp", "fsdp"),
        P("tp", "fsdp"),
        P(),
        P(),
    )
    out_specs = (
        P("tp", "fsdp", None),
        P("tp", "fsdp", None),
        P("tp", "fsdp"),
        P("tp", "fsdp"),
        P("tp", "fsdp"),
        P("tp", "fsdp"),
        P(),
        P(),
        P(),
    )
    return jax.shard_map(on_device, mesh=mesh, in_specs=in_specs, out_specs=out_specs, check_vma=False)
```

```python
from functools import partial

import jax
import jax.numpy as jnp
from jax import lax
from jax.experimental import pallas as pl
from jax.experimental.pallas import tpu as pltpu
from jax.sharding import PartitionSpec as P


HD = 64
LANES = 128
SCALE = 0.125
EPS = 1e-12
NEG = -1e30
RSQRT2 = 0.7071067811865476
RSQRT2PI = 0.3989422804014327
F32 = jnp.float32
BF16 = jnp.bfloat16


def dot_nn(a, b):
    return lax.dot_general(a, b, (((1,), (0,)), ((), ())), preferred_element_type=F32)


def dot_nt(a, b):
    return lax.dot_general(a, b, (((1,), (1,)), ((), ())), preferred_element_type=F32)


def dot_tn(a, b):
    return lax.dot_general(a, b, (((0,), (0,)), ((), ())), preferred_element_type=F32)


def pack(value):
    half = value.shape[0] // 2
    tail = value[:, LANES:]
    return jnp.concatenate(
        [value[:, :LANES], jnp.concatenate([tail[:half], tail[half:]], axis=1)], axis=0
    )


def unpack(block):
    rows = block.shape[0] * 2 // 3
    tail = block[rows:]
    return jnp.concatenate(
        [block[:rows], jnp.concatenate([tail[:, :HD], tail[:, HD:]], axis=0)], axis=1
    )


def lay_pairs(near, other, first, emit):
    for z in range(near.shape[0]):
        own, far = near[z], other[z]
        emit(2 * z, jnp.where(first, own, far))
        emit(2 * z + 1, jnp.where(first, far, own))


def fold_lanes(value):
    half = value.shape[1] // 2
    return jnp.concatenate([value[:, :half], value[:, half:]], axis=0)


def unfold_lanes(value):
    half = value.shape[0] // 2
    return jnp.concatenate([value[:half], value[half:]], axis=1)


def small_rows(count):
    return (count // 2 + 7) // 8 * 8


def fold_small(value):
    top = small_rows(value.shape[0])
    lower = value[top:]
    fill = jnp.zeros((2 * top - value.shape[0], value.shape[1]), value.dtype)
    return jnp.concatenate([value[:top], jnp.concatenate([lower, fill], axis=0)], axis=1)


def prepare_kernel(out_ref, in_ref, down_ref, block_ref):
    wide = jnp.concatenate([out_ref[...].astype(F32).T, in_ref[...].astype(F32).T], axis=1)
    deep = fold_lanes(down_ref[...].astype(F32))
    block = jnp.concatenate([wide, deep], axis=0).astype(BF16)
    for z in range(block_ref.shape[0]):
        block_ref[z] = block


def split_kernel(place_ref, tok_ref, tok_out, *rest):
    sends, held = rest[:-1], rest[-1]
    groups = len(sends)
    width = tok_ref.shape[2] // groups
    for n in range(tok_ref.shape[1]):
        rows = tok_ref[:, n, :]
        tok_out[n] = rows
        for g in range(groups):
            held[g, n] = pack(rows[:, g * width : (g + 1) * width])
    for s in range(groups):
        sends[s][...] = held[place_ref[0] ^ s]


def part_kernel(in_ref, out_ref):
    for n in range(in_ref.shape[1]):
        out_ref[n] = in_ref[:, n, :]


def merge_kernel(in_ref, out_ref):
    for n in range(in_ref.shape[0]):
        out_ref[:, n, :] = in_ref[n]


def join_kernel(place_ref, mix_ref, *rest):
    backs, out_ref, held = rest[:-2], rest[-2], rest[-1]
    sequences = mix_ref.shape[0]
    groups = len(backs) // sequences
    for n in range(sequences):
        for s in range(groups):
            held[place_ref[0] ^ s, n] = backs[n * groups + s][...]
    for n in range(sequences):
        pulled = jnp.concatenate([unpack(held[g, n]) for g in range(groups)], axis=1)
        out_ref[:, n, :] = mix_ref[n] + pulled.astype(F32)


def load_heads(place_ref, chunk_refs, qkv_ref, tokens, weight, parts_ref, n, block):
    count = qkv_ref.shape[1]
    for f in range(qkv_ref.shape[0]):
        weight[f * count : (f + 1) * count] = qkv_ref[f]
    for s in range(len(chunk_refs)):
        start = pl.multiple_of((place_ref[0] ^ s) * block, block)
        tokens[pl.ds(start, block)] = unpack(chunk_refs[s][n])
    projected = dot_nt(tokens[...], weight[...]).astype(BF16)
    for i in range(parts_ref.shape[0]):
        parts_ref[i] = projected[:, i * HD : (i + 1) * HD]


def masked_scores(keys, query, length):
    raw = dot_nt(keys, query)
    span, block = raw.shape
    edge = span - block
    spot = lax.broadcasted_iota(jnp.int32, (block, block), 0) + edge
    last = jnp.where(spot < length, raw[edge:], NEG)
    return jnp.concatenate([raw[:edge], last], axis=0) if edge else last


def for_span(length, block, parts, body):
    for count in range(1, parts + 1):
        span = count * block
        pl.when((length > span - block) & (length <= span))(partial(body, count, span))


def attend_kernel(len_ref, place_ref, *rest, block, parts, n):
    chunk_refs, qkv_ref, rest = rest[:parts], rest[parts], rest[parts + 1 :]
    sends, (lse_ref, weight, tokens, pieces, mixed, held) = rest[:parts], rest[parts:]
    length = len_ref[n]
    heads = pieces.shape[0] // 3
    load_heads(place_ref, chunk_refs, qkv_ref, tokens, weight, pieces, n, block)
    mixed[...] = jnp.zeros_like(mixed)
    lse_ref[...] = jnp.zeros_like(lse_ref)

    def body(count, span):
        @pl.loop(0, heads)
        def _(h):
            values_t = pieces[2 * heads + h, 0:span].T

            @pl.loop(0, count)
            def _(b):
                at = pl.ds(pl.multiple_of(b * block, block), block)
                query = (pieces[h, at] * SCALE).astype(BF16)
                masked = masked_scores(pieces[heads + h, 0:span], query, length)
                top = jnp.max(masked, axis=0, keepdims=True)
                terms = jnp.exp(masked - top)
                total = jnp.sum(terms, axis=0, keepdims=True)
                mixed[h, at] = (dot_nn(values_t, terms.astype(BF16)) / total).T.astype(BF16)
                lse_ref[h, b] = top + jnp.log(total)

    for_span(length, block, parts, body)
    for i in range(parts):
        rows = slice(i * block, (i + 1) * block)
        held[i] = pack(jnp.concatenate([mixed[h, rows] for h in range(heads)], axis=1))
    for s in range(parts):
        sends[s][...] = held[place_ref[0] ^ s]


def attend_back_kernel(len_ref, place_ref, *rest, block, parts, n, last_call):
    chunk_refs, g_refs, ctx_refs = rest[:parts], rest[parts : 2 * parts], rest[2 * parts : 3 * parts]
    qkv_ref, lse_ref, rest = rest[3 * parts], rest[3 * parts + 1], rest[3 * parts + 2 :]
    if last_call:
        start_ref, rest = rest[0], rest[1:]
    sends, rest = rest[:parts], rest[parts:]
    if last_call:
        keep_ref, send_ref, rest = rest[0], rest[1], rest[2:]
    dw, weight, tokens, pieces, dpieces, grad, delta, dk, dv, held = rest
    length = len_ref[n]
    heads = pieces.shape[0] // 3
    shards = qkv_ref.shape[0]
    load_heads(place_ref, chunk_refs, qkv_ref, tokens, weight, pieces, n, block)
    for s in range(parts):
        spot = place_ref[0] ^ s
        at = pl.ds(pl.multiple_of(spot * block, block), block)
        piece = unpack(g_refs[s][...])
        both_t = (piece.astype(F32) * unpack(ctx_refs[s][...]).astype(F32)).T
        for h in range(heads):
            grad[h, at] = piece[:, h * HD : (h + 1) * HD]
            delta[h, spot] = jnp.sum(both_t[h * HD : (h + 1) * HD], axis=0, keepdims=True)
    dpieces[...] = jnp.zeros_like(dpieces)

    def body(count, span):
        @pl.loop(0, heads)
        def _(h):
            keys_t = pieces[heads + h, 0:span].T
            dk[...] = jnp.zeros_like(dk)
            dv[...] = jnp.zeros_like(dv)

            @pl.loop(0, count)
            def _(b):
                at = pl.ds(pl.multiple_of(b * block, block), block)
                query = (pieces[h, at] * SCALE).astype(BF16)
                upstream = grad[h, at]
                probs = jnp.exp(masked_scores(pieces[heads + h, 0:span], query, length) - lse_ref[h, b])
                dprobs = dot_nt(pieces[2 * heads + h, 0:span], upstream)
                dscores = (probs * (dprobs - delta[h, b])).astype(BF16)
                dv[0:span] += dot_nn(probs.astype(BF16), upstream)
                dk[0:span] += dot_nn(dscores, query)
                dpieces[h, at] = (dot_nn(keys_t, dscores) * SCALE).T.astype(BF16)

            dpieces[heads + h, 0:span] = dk[0:span].astype(BF16)
            dpieces[2 * heads + h, 0:span] = dv[0:span].astype(BF16)

    for_span(length, block, parts, body)
    dprojected = jnp.concatenate([dpieces[i] for i in range(3 * heads)], axis=1)
    back = dot_nn(dprojected, weight[...]).astype(BF16)
    for i in range(parts):
        held[i] = pack(back[i * block : (i + 1) * block])
    for s in range(parts):
        sends[s][...] = held[place_ref[0] ^ s]
    total = dot_tn(dprojected, tokens[...])
    if not last_call:
        dw[...] = total
        return
    dw[...] = total + start_ref[...]
    count = dw.shape[0] // shards
    first = place_ref[1] == 0
    for z in range(shards // 2):
        even = fold_small(dw[2 * z * count : (2 * z + 1) * count])
        odd = fold_small(dw[(2 * z + 1) * count : (2 * z + 2) * count])
        keep_ref[z] = jnp.where(first, even, odd).astype(BF16)
        send_ref[z] = jnp.where(first, odd, even).astype(BF16)


def plus(a, b):
    return (a.astype(F32) + b.astype(F32)).astype(BF16)


def fold_core_kernel(wide, wide_in, deep, deep_in, stat, stat_in, wide_keep, wide_send, deep_keep, deep_send, stat_out):
    for y in range(2):
        wide_keep[y] = plus(wide[y, 0], wide_in[y, 0])
        wide_send[y] = plus(wide[y, 1], wide_in[y, 1])
    for x in range(2):
        deep_keep[x] = plus(deep[0, x], deep_in[0, x])
        deep_send[x] = plus(deep[1, x], deep_in[1, x])
    stat_out[...] = stat[...] + stat_in[...]


def fold_link_kernel(wide, wide_in, deep, deep_in, stat, stat_in, wide_keep, wide_send, deep_keep, deep_send, stat_out):
    wide_keep[...] = plus(wide[0], wide_in[0])
    wide_send[...] = plus(wide[1], wide_in[1])
    deep_keep[...] = plus(deep[0], deep_in[0])
    deep_send[...] = plus(deep[1], deep_in[1])
    stat_out[...] = stat[...] + stat_in[...]


def fold_far_kernel(wide, wide_in, deep, deep_in, small, small_in, stat, stat_in, block_ref):
    stats = stat[...] + stat_in[...]
    high = stats.astype(BF16)
    stats = jnp.concatenate([high.astype(F32), stats - high.astype(F32)], axis=0)
    stats = fold_lanes(stats).astype(BF16)
    edge = 0
    for ours, theirs in ((wide, wide_in), (deep, deep_in), (small, small_in)):
        count = ours.shape[1]
        block_ref[:, edge : edge + count] = plus(ours[...], theirs[...])
        edge += count
    for z in range(block_ref.shape[0]):
        block_ref[z, edge:] = stats


def finish_kernel(block_ref, d_qkv, d_out, d_in, d_down, gains_ref, biases_ref, rms_ref, total):
    acc = block_ref[0].astype(F32)
    for z in range(1, block_ref.shape[0]):
        acc = acc + block_ref[z].astype(F32)
    total[...] = acc
    width, wide_rows = d_out.shape
    d_out[...] = total[0:wide_rows, :width].T
    d_in[...] = total[0:wide_rows, width:].T
    edge = wide_rows + 2 * d_down.shape[0]
    d_down[...] = unfold_lanes(total[wide_rows:edge])
    count = d_qkv.shape[0]
    top = small_rows(count)
    small = total[edge : edge + top]
    d_qkv[...] = jnp.concatenate([small[:, :width], small[: count - top, width:]], axis=0)
    stats = unfold_lanes(total[edge + top :])
    stats = stats[:8] + stats[8:]
    gains_ref[...] = stats[0:2]
    biases_ref[...] = stats[2:4]
    count = jnp.max(stats[7:8], axis=1, keepdims=True)
    square = jnp.sum(stats[4:7], axis=1, keepdims=True)
    means = jnp.sqrt(square / (count * stats.shape[1]))
    here = lax.broadcasted_iota(jnp.int32, (3, 3), 0) == lax.broadcasted_iota(jnp.int32, (3, 3), 1)
    rms_ref[...] = jnp.sum(jnp.where(here, jnp.broadcast_to(means, (3, 3)), 0.0), axis=0, keepdims=True)


def mean_of(value):
    return jnp.mean(value, axis=-1, keepdims=True)


def col_sum(value):
    return jnp.sum(value, axis=0, keepdims=True)


def gelu_pair(pre):
    upper = 0.5 * (1.0 + lax.erf(pre * RSQRT2))
    slope = upper + pre * (jnp.exp(-0.5 * pre * pre) * RSQRT2PI)
    return pre * upper, slope


def middle_kernel(len_ref, place_ref, *rest, groups, sequences):
    ctx_refs, rest = rest[: groups * sequences], rest[groups * sequences :]
    tok_ref, cot_ref, gain_ref, bias_ref, rest = *rest[:4], rest[4:]
    wides, deeps, rest = rest[:8], rest[8:16], rest[16:]
    out_ref, mix_ref, rest = rest[0], rest[1], rest[2:]
    sends, rest = rest[: groups * sequences], rest[groups * sequences :]
    keep_w, send_w, keep_d, send_d, stats, w_out, w_in, w_down, hid, slope, acc_a, acc_d, held = rest
    place = place_ref[0]
    first = place_ref[1] == 0
    rows = tok_ref.shape[1]
    model = tok_ref.shape[2]
    width = model // groups
    shards = 2 * wides[0].shape[0]
    wide_rows, deep_rows = model // shards, width // shards

    for core in range(2):
        for y in range(2):
            g = place ^ (2 * y + core)

            def lay_wide(f, block):
                w_out[g, f * wide_rows : (f + 1) * wide_rows] = block[:, :width]
                w_in[g, f * wide_rows : (f + 1) * wide_rows] = block[:, width:]

            def lay_deep(f, block):
                w_down[g, f * deep_rows : (f + 1) * deep_rows] = unfold_lanes(block)

            lay_pairs(wides[core * 4 + y * 2], wides[core * 4 + y * 2 + 1], first, lay_wide)
            lay_pairs(deeps[core * 4 + y * 2], deeps[core * 4 + y * 2 + 1], first, lay_deep)
    for n in range(sequences):
        for s in range(groups):
            held[n, s] = ctx_refs[n * groups + s][...]
    acc_a[...] = jnp.zeros_like(acc_a)
    acc_d[...] = jnp.zeros_like(acc_d)
    stats[...] = jnp.zeros_like(stats)
    gain0, gain1 = gain_ref[0:1, :], gain_ref[1:2, :]
    bias0, bias1 = bias_ref[0:1, :], bias_ref[1:2, :]

    @pl.loop(0, sequences)
    def _(n):
        spot = lax.broadcasted_iota(jnp.int32, (rows, 1), 0) + place * rows
        valid = (spot < len_ref[n]).astype(F32)
        tokens = tok_ref[n].astype(F32)
        contexts = [unpack(held[n, s]) for s in range(groups)]
        attention = dot_nt(contexts[0], w_out[place])
        for s in range(1, groups):
            attention = attention + dot_nt(contexts[s], w_out[place ^ s])
        mixed = tokens + attention
        centered = mixed - mean_of(mixed)
        inv0 = lax.rsqrt(mean_of(centered * centered) + EPS)
        xhat0 = centered * inv0
        first = xhat0 * gain0 + bias0
        ffn_in = first.astype(BF16)
        pieces = []
        for g in range(groups):
            cols = slice(g * width, (g + 1) * width)
            pre = dot_nt(ffn_in[:, cols], w_in[g])
            hidden, tilt = gelu_pair(pre)
            hidden = hidden.astype(BF16)
            hid[g] = hidden
            slope[g] = tilt
            pieces.append(dot_nt(hidden, w_down[g]))
        ffn = jnp.concatenate(pieces, axis=1).astype(BF16).astype(F32)
        second = first + ffn
        centered = second - mean_of(second)
        inv1 = lax.rsqrt(mean_of(centered * centered) + EPS)
        xhat1 = centered * inv1
        out_ref[n] = ((xhat1 * gain1 + bias1) * valid).astype(BF16)
        upstream = cot_ref[n].astype(F32) * valid
        scaled = upstream * gain1
        g_second = inv1 * (scaled - mean_of(scaled) - xhat1 * mean_of(scaled * xhat1))
        g_ffn = g_second.astype(BF16)
        pieces = []
        for g in range(groups):
            cols = slice(g * width, (g + 1) * width)
            g_hidden = dot_nn(g_ffn[:, cols], w_down[g]).astype(BF16).astype(F32)
            g_pre = (g_hidden * slope[g]).astype(BF16)
            acc_d[g] += dot_tn(g_ffn[:, cols], hid[g])
            acc_a[1, g] += dot_tn(g_pre, ffn_in[:, cols])
            pieces.append(dot_nn(g_pre, w_in[g]))
        g_input = jnp.concatenate(pieces, axis=1).astype(BF16).astype(F32)
        upper = g_second + g_input
        scaled = upper * gain0
        g_mix = inv0 * (scaled - mean_of(scaled) - xhat0 * mean_of(scaled * xhat0))
        mix_ref[n] = g_mix
        g_attn = g_mix.astype(BF16)
        for s in range(groups):
            acc_a[0, place ^ s] += dot_tn(g_attn, contexts[s])
            held[n, s] = pack(dot_nn(g_attn, w_out[place ^ s]).astype(BF16))
        stats[0:1] += col_sum(upper * xhat0)
        stats[1:2] += col_sum(upstream * xhat1)
        stats[2:3] += col_sum(upper)
        stats[3:4] += col_sum(upstream)
        stats[4:5] += col_sum(tokens * tokens * valid)
        stats[5:6] += col_sum(attention * attention * valid)
        stats[6:7] += col_sum(ffn * ffn * valid)
        stats[7:8] += jnp.broadcast_to(jnp.sum(valid, axis=0, keepdims=True), (1, model))

    for n in range(sequences):
        for s in range(groups):
            sends[n * groups + s][...] = held[n, s]
    for core, (wide, deep) in enumerate(((keep_w, keep_d), (send_w, send_d))):
        for y in range(2):
            g = place ^ (2 * y + core)
            for z in range(shards // 2):
                blocks = []
                for f in (2 * z, 2 * z + 1):
                    at = slice(f * wide_rows, (f + 1) * wide_rows)
                    down = acc_d[g, f * deep_rows : (f + 1) * deep_rows]
                    blocks.append((jnp.concatenate([acc_a[0, g, at], acc_a[1, g, at]], axis=1), fold_lanes(down)))
                for x in range(2):
                    wide[y, x, z] = jnp.where(first, blocks[x][0], blocks[1 - x][0]).astype(BF16)
                    deep[y, x, z] = jnp.where(first, blocks[x][1], blocks[1 - x][1]).astype(BF16)


def flip(value, axis, bit):
    size = lax.axis_size(axis)
    return lax.ppermute(value, axis, [(i, i ^ bit) for i in range(size)])


def tp_exchange(chunks):
    order = sorted(range(1, len(chunks)), reverse=True)
    moved = {s: flip(chunks[s], "tp", s) for s in order}
    return [chunks[0]] + [moved[s] for s in range(1, len(chunks))]


def far_exchange(value):
    groups = [list(range(bit, lax.axis_size("fsdp"), 2)) for bit in range(2)]
    return lax.all_to_all(value, "fsdp", 0, 0, axis_index_groups=groups)


def on_device(tokens, cotangent, lengths, qkv_weight, out_weight, in_weight, down_weight, gains, biases):
    groups = lax.axis_size("tp")
    shards = lax.axis_size("fsdp")
    place = jnp.stack([lax.axis_index("tp"), lax.axis_index("fsdp") % 2]).astype(jnp.int32)
    rows, sequences, model = tokens.shape
    width = model // groups
    hidden = in_weight.shape[1] * shards
    positions = rows * groups
    packed = rows * 3 // 2
    far = shards // 2
    wide_rows, deep_rows, small = model // shards, 2 * width // shards, small_rows(3 * width // shards)
    vmem = pl.BlockSpec(memory_space=pltpu.VMEM)
    smem = pl.BlockSpec(memory_space=pltpu.SMEM)

    def shape(dims, kind=BF16):
        return jax.ShapeDtypeStruct(dims, kind)

    def call(kernel, outs, *operands, scalars=0, scratch=()):
        return pl.pallas_call(
            kernel,
            out_shape=outs,
            in_specs=[smem] * scalars + [vmem] * (len(operands) - scalars),
            out_specs=jax.tree.map(lambda _: vmem, outs),
            scratch_shapes=list(scratch),
        )(*operands)

    one = shape((packed, LANES))
    both = shape((sequences, packed, LANES))
    by_sequence = shape((sequences, rows, model))

    edge = wide_rows + deep_rows
    qkv_block = qkv_weight.T
    qkv = lax.all_to_all(jnp.broadcast_to(qkv_block[None], (shards,) + qkv_block.shape), "fsdp", 0, 0)
    tok_rows, *grouped = call(
        split_kernel,
        (by_sequence,) + (both,) * groups,
        place,
        tokens,
        scalars=1,
        scratch=[pltpu.VMEM((groups, sequences, packed, LANES), BF16)],
    )
    grouped = tp_exchange(grouped)
    sent = call(prepare_kernel, shape((far, edge, 2 * width)), out_weight, in_weight, down_weight.T)
    near = far_exchange(sent)
    cot_rows = call(part_kernel, by_sequence, cotangent)
    wide, deep = near[:, :wide_rows], near[:, wide_rows:]
    wide_y = flip(wide, "tp", 2)
    deep_x = flip(deep, "fsdp", 1)
    wides = [wide, flip(wide, "fsdp", 1), wide_y, flip(wide_y, "fsdp", 1)]
    deeps = [deep, deep_x, flip(deep, "tp", 2), flip(deep_x, "tp", 2)]
    wides += [flip(value, "tp", 1) for value in wides]
    deeps += [flip(value, "tp", 1) for value in deeps]

    heads = width // HD
    lse, context, mine = [], [], []
    for n in range(sequences):
        *chunks, sums = call(
            partial(attend_kernel, block=rows, parts=groups, n=n),
            (one,) * groups + (shape((heads, groups, 1, rows), F32),),
            lengths,
            place,
            *grouped,
            qkv,
            scalars=2,
            scratch=[
                pltpu.VMEM((3 * width, width), BF16),
                pltpu.VMEM((positions, width), BF16),
                pltpu.VMEM((3 * heads, positions, HD), BF16),
                pltpu.VMEM((heads, positions, HD), BF16),
                pltpu.VMEM((groups, packed, LANES), BF16),
            ],
        )
        lse.append(sums)
        context.append(chunks)
        mine += tp_exchange(chunks)

    half_w = shape((2, 2, far, wide_rows, 2 * width))
    half_d = shape((2, 2, far, deep_rows, 2 * width))
    out_rows, g_mix, *rest = call(
        partial(middle_kernel, groups=groups, sequences=sequences),
        (by_sequence, shape((sequences, rows, model), F32))
        + (one,) * (groups * sequences)
        + (half_w, half_w, half_d, half_d, shape((8, model), F32)),
        lengths,
        place,
        *mine,
        tok_rows,
        cot_rows,
        gains,
        biases,
        *wides,
        *deeps,
        scalars=2,
        scratch=[
            pltpu.VMEM((groups, model, width), BF16),
            pltpu.VMEM((groups, hidden, width), BF16),
            pltpu.VMEM((groups, width, hidden), BF16),
            pltpu.VMEM((groups, rows, hidden), BF16),
            pltpu.VMEM((groups, rows, hidden), F32),
            pltpu.VMEM((2, groups, model, width), F32),
            pltpu.VMEM((groups, width, hidden), F32),
            pltpu.VMEM((sequences, groups, packed, LANES), BF16),
        ],
    )
    upstream = [tp_exchange(rest[n * groups : (n + 1) * groups]) for n in range(sequences)]
    keep_w, send_w, keep_d, send_d, stats = rest[groups * sequences :]
    output = call(merge_kernel, shape(tokens.shape), out_rows)

    pair_w, pair_d = shape(half_w.shape[1:]), shape(half_d.shape[1:])
    part_w, part_d = shape(half_w.shape[2:]), shape(half_d.shape[2:])
    sums = shape(stats.shape, F32)
    keep_w, send_w, keep_d, send_d, stats = call(
        fold_core_kernel,
        (pair_w, pair_w, pair_d, pair_d, sums),
        keep_w,
        flip(send_w, "tp", 1),
        keep_d,
        flip(send_d, "tp", 1),
        stats,
        flip(stats, "tp", 1),
    )
    keep_w, send_w, keep_d, send_d, stats = call(
        fold_link_kernel,
        (part_w, part_w, part_d, part_d, sums),
        keep_w,
        flip(send_w, "fsdp", 1),
        keep_d,
        flip(send_d, "tp", 2),
        stats,
        flip(stats, "fsdp", 1),
    )
    wide_in = flip(send_w, "tp", 2)
    deep_in = flip(send_d, "fsdp", 1)
    stats_in = flip(stats, "tp", 2)

    back, d_qkv = [], []
    for n in range(sequences):
        last = n == sequences - 1
        quarter = shape((far, small, 2 * width))
        full = shape((3 * width, width), F32)
        scratch = [
            pltpu.VMEM((3 * width, width), BF16),
            pltpu.VMEM((positions, width), BF16),
            pltpu.VMEM((3 * heads, positions, HD), BF16),
            pltpu.VMEM((3 * heads, positions, HD), BF16),
            pltpu.VMEM((heads, positions, HD), BF16),
            pltpu.VMEM((heads, groups, 1, rows), F32),
            pltpu.VMEM((positions, HD), F32),
            pltpu.VMEM((positions, HD), F32),
            pltpu.VMEM((groups, packed, LANES), BF16),
        ]
        outs = (one,) * groups + ((quarter, quarter) if last else (full,))
        if last:
            scratch.insert(0, pltpu.VMEM((3 * width, width), F32))
        *chunks, = call(
            partial(attend_back_kernel, block=rows, parts=groups, n=n, last_call=last),
            outs,
            lengths,
            place,
            *grouped,
            *upstream[n],
            *context[n],
            qkv,
            lse[n],
            *d_qkv,
            scalars=2,
            scratch=scratch,
        )
        d_qkv = chunks[groups:]
        back += tp_exchange(chunks[:groups])
    keep_q, send_q = d_qkv

    blocks = call(
        fold_far_kernel,
        shape((far, edge + small + 32, 2 * width)),
        keep_w,
        wide_in,
        keep_d,
        deep_in,
        keep_q,
        flip(send_q, "fsdp", 1),
        stats,
        stats_in,
    )
    blocks = far_exchange(blocks)
    d_input = call(
        join_kernel,
        shape(tokens.shape, F32),
        place,
        g_mix,
        *back,
        scalars=1,
        scratch=[pltpu.VMEM((groups, sequences, packed, LANES), BF16)],
    )
    d_qkv, d_out, d_in, d_down, d_gains, d_biases, rms = call(
        finish_kernel,
        (
            shape(qkv_block.shape, F32),
            shape(out_weight.shape, F32),
            shape(in_weight.shape, F32),
            shape(down_weight.shape[::-1], F32),
            shape(gains.shape, F32),
            shape(biases.shape, F32),
            shape((1, 3), F32),
        ),
        blocks,
        scratch=[pltpu.VMEM(blocks.shape[1:], F32)],
    )
    return output, d_input, d_qkv.T, d_out, d_in, d_down.T, d_gains, d_biases, rms[0]


def solution(mesh):
    in_specs = (
        P("tp", "fsdp", None),
        P("tp", "fsdp", None),
        P("fsdp"),
        P("tp", "fsdp"),
        P("tp", "fsdp"),
        P("tp", "fsdp"),
        P("tp", "fsdp"),
        P(),
        P(),
    )
    out_specs = (
        P("tp", "fsdp", None),
        P("tp", "fsdp", None),
        P("tp", "fsdp"),
        P("tp", "fsdp"),
        P("tp", "fsdp"),
        P("tp", "fsdp"),
        P(),
        P(),
        P(),
    )
    return jax.shard_map(
        on_device, mesh=mesh, in_specs=in_specs, out_specs=out_specs, check_vma=False
    )
```

```python
from functools import partial

import jax
import jax.numpy as jnp
from jax import lax
from jax.experimental import pallas as pl
from jax.experimental.pallas import tpu as pltpu
from jax.sharding import PartitionSpec as P


HD = 64
LANES = 128
SCALE = 0.125
EPS = 1e-12
NEG = -1e30
RSQRT2 = 0.7071067811865476
RSQRT2PI = 0.3989422804014327
F32 = jnp.float32
BF16 = jnp.bfloat16


def dot_nn(a, b):
    return lax.dot_general(a, b, (((1,), (0,)), ((), ())), preferred_element_type=F32)


def dot_nt(a, b):
    return lax.dot_general(a, b, (((1,), (1,)), ((), ())), preferred_element_type=F32)


def dot_tn(a, b):
    return lax.dot_general(a, b, (((0,), (0,)), ((), ())), preferred_element_type=F32)


def pack(value):
    half = value.shape[0] // 2
    tail = value[:, LANES:]
    return jnp.concatenate(
        [value[:, :LANES], jnp.concatenate([tail[:half], tail[half:]], axis=1)], axis=0
    )


def unpack(block):
    rows = block.shape[0] * 2 // 3
    tail = block[rows:]
    return jnp.concatenate(
        [block[:rows], jnp.concatenate([tail[:, :HD], tail[:, HD:]], axis=0)], axis=1
    )


def lay_pairs(near, other, first, emit):
    for z in range(near.shape[0]):
        own, far = near[z], other[z]
        emit(2 * z, jnp.where(first, own, far))
        emit(2 * z + 1, jnp.where(first, far, own))


def fold_lanes(value):
    half = value.shape[1] // 2
    return jnp.concatenate([value[:, :half], value[:, half:]], axis=0)


def unfold_lanes(value):
    half = value.shape[0] // 2
    return jnp.concatenate([value[:half], value[half:]], axis=1)


def small_rows(count):
    return (count // 2 + 7) // 8 * 8


def fold_small(value):
    top = small_rows(value.shape[0])
    lower = value[top:]
    fill = jnp.zeros((2 * top - value.shape[0], value.shape[1]), value.dtype)
    return jnp.concatenate([value[:top], jnp.concatenate([lower, fill], axis=0)], axis=1)


def prepare_kernel(qkv_ref, out_ref, in_ref, down_ref, block_ref):
    wide = jnp.concatenate([out_ref[...].astype(F32).T, in_ref[...].astype(F32).T], axis=1)
    deep = fold_lanes(down_ref[...].astype(F32))
    small = fold_small(qkv_ref[...].astype(F32))
    block = jnp.concatenate([wide, deep, small], axis=0).astype(BF16)
    for z in range(block_ref.shape[0]):
        block_ref[z] = block


def split_kernel(place_ref, tok_ref, tok_out, *rest):
    sends, held = rest[:-1], rest[-1]
    groups = len(sends)
    width = tok_ref.shape[2] // groups
    for n in range(tok_ref.shape[1]):
        rows = tok_ref[:, n, :]
        tok_out[n] = rows
        for g in range(groups):
            held[g, n] = pack(rows[:, g * width : (g + 1) * width])
    for s in range(groups):
        sends[s][...] = held[place_ref[0] ^ s]


def part_kernel(in_ref, out_ref):
    for n in range(in_ref.shape[1]):
        out_ref[n] = in_ref[:, n, :]


def merge_kernel(in_ref, out_ref):
    for n in range(in_ref.shape[0]):
        out_ref[:, n, :] = in_ref[n]


def join_kernel(place_ref, mix_ref, *rest):
    backs, out_ref, held = rest[:-2], rest[-2], rest[-1]
    sequences = mix_ref.shape[0]
    groups = len(backs) // sequences
    for n in range(sequences):
        for s in range(groups):
            held[place_ref[0] ^ s, n] = backs[n * groups + s][...]
    for n in range(sequences):
        pulled = jnp.concatenate([unpack(held[g, n]) for g in range(groups)], axis=1)
        out_ref[:, n, :] = mix_ref[n] + pulled.astype(F32)


def load_heads(place_ref, chunk_refs, qkv_refs, tokens, weight, parts_ref, n, block):
    near_ref, other_ref = qkv_refs
    count = weight.shape[0] // (2 * near_ref.shape[0])
    top = small_rows(count)

    def lay_small(f, value):
        half = value.shape[1] // 2
        weight[f * count : f * count + top] = value[:, :half]
        weight[f * count + top : (f + 1) * count] = value[: count - top, half:]

    lay_pairs(near_ref, other_ref, place_ref[1] == 0, lay_small)
    for s in range(len(chunk_refs)):
        start = pl.multiple_of((place_ref[0] ^ s) * block, block)
        tokens[pl.ds(start, block)] = unpack(chunk_refs[s][n])
    projected = dot_nt(tokens[...], weight[...]).astype(BF16)
    for i in range(parts_ref.shape[0]):
        parts_ref[i] = projected[:, i * HD : (i + 1) * HD]


def masked_scores(keys, query, length):
    raw = dot_nt(keys, query)
    span, block = raw.shape
    edge = span - block
    spot = lax.broadcasted_iota(jnp.int32, (block, block), 0) + edge
    last = jnp.where(spot < length, raw[edge:], NEG)
    return jnp.concatenate([raw[:edge], last], axis=0) if edge else last


def for_span(length, block, parts, body):
    for count in range(1, parts + 1):
        span = count * block
        pl.when((length > span - block) & (length <= span))(partial(body, count, span))


def attend_kernel(len_ref, place_ref, *rest, block, parts, n):
    chunk_refs, qkv_refs, rest = rest[:parts], rest[parts : parts + 2], rest[parts + 2 :]
    sends, (lse_ref, weight, tokens, pieces, mixed, held) = rest[:parts], rest[parts:]
    length = len_ref[n]
    heads = pieces.shape[0] // 3
    load_heads(place_ref, chunk_refs, qkv_refs, tokens, weight, pieces, n, block)
    mixed[...] = jnp.zeros_like(mixed)
    lse_ref[...] = jnp.zeros_like(lse_ref)

    def body(count, span):
        @pl.loop(0, heads)
        def _(h):
            values_t = pieces[2 * heads + h, 0:span].T

            for b in range(count):
                at = slice(b * block, (b + 1) * block)
                query = (pieces[h, at] * SCALE).astype(BF16)
                masked = masked_scores(pieces[heads + h, 0:span], query, length)
                top = jnp.max(masked, axis=0, keepdims=True)
                terms = jnp.exp(masked - top)
                total = jnp.sum(terms, axis=0, keepdims=True)
                mixed[h, at] = (dot_nn(values_t, terms.astype(BF16)) / total).T.astype(BF16)
                lse_ref[h, b] = top + jnp.log(total)

    for_span(length, block, parts, body)
    for i in range(parts):
        rows = slice(i * block, (i + 1) * block)
        held[i] = pack(jnp.concatenate([mixed[h, rows] for h in range(heads)], axis=1))
    for s in range(parts):
        sends[s][...] = held[place_ref[0] ^ s]


def attend_back_kernel(len_ref, place_ref, *rest, block, parts, n, last_call):
    chunk_refs, g_refs, ctx_refs = rest[:parts], rest[parts : 2 * parts], rest[2 * parts : 3 * parts]
    qkv_refs, lse_ref, rest = rest[3 * parts : 3 * parts + 2], rest[3 * parts + 2], rest[3 * parts + 3 :]
    if last_call:
        start_ref, rest = rest[0], rest[1:]
    sends, rest = rest[:parts], rest[parts:]
    if last_call:
        keep_ref, send_ref, rest = rest[0], rest[1], rest[2:]
    dw, weight, tokens, pieces, dpieces, grad, delta, held = rest
    length = len_ref[n]
    heads = pieces.shape[0] // 3
    shards = 2 * qkv_refs[0].shape[0]
    load_heads(place_ref, chunk_refs, qkv_refs, tokens, weight, pieces, n, block)
    for s in range(parts):
        spot = place_ref[0] ^ s
        at = pl.ds(pl.multiple_of(spot * block, block), block)
        piece = unpack(g_refs[s][...])
        both_t = (piece.astype(F32) * unpack(ctx_refs[s][...]).astype(F32)).T
        for h in range(heads):
            grad[h, at] = piece[:, h * HD : (h + 1) * HD]
            delta[h, spot] = jnp.sum(both_t[h * HD : (h + 1) * HD], axis=0, keepdims=True)
    dpieces[...] = jnp.zeros_like(dpieces)

    def body(count, span):
        @pl.loop(0, heads)
        def _(h):
            keys_t = pieces[heads + h, 0:span].T
            sum_k = sum_v = jnp.zeros((span, HD), F32)
            for b in range(count):
                at = slice(b * block, (b + 1) * block)
                query = (pieces[h, at] * SCALE).astype(BF16)
                upstream = grad[h, at]
                probs = jnp.exp(masked_scores(pieces[heads + h, 0:span], query, length) - lse_ref[h, b])
                dprobs = dot_nt(pieces[2 * heads + h, 0:span], upstream)
                dscores = (probs * (dprobs - delta[h, b])).astype(BF16)
                sum_v = sum_v + dot_nn(probs.astype(BF16), upstream)
                sum_k = sum_k + dot_nn(dscores, query)
                dpieces[h, at] = (dot_nn(keys_t, dscores) * SCALE).T.astype(BF16)

            dpieces[heads + h, 0:span] = sum_k.astype(BF16)
            dpieces[2 * heads + h, 0:span] = sum_v.astype(BF16)

    for_span(length, block, parts, body)
    dprojected = jnp.concatenate([dpieces[i] for i in range(3 * heads)], axis=1)
    back = dot_nn(dprojected, weight[...]).astype(BF16)
    for i in range(parts):
        held[i] = pack(back[i * block : (i + 1) * block])
    for s in range(parts):
        sends[s][...] = held[place_ref[0] ^ s]
    total = dot_tn(dprojected, tokens[...])
    if not last_call:
        dw[...] = total
        return
    dw[...] = total + start_ref[...]
    count = dw.shape[0] // shards
    first = place_ref[1] == 0
    for z in range(shards // 2):
        even = fold_small(dw[2 * z * count : (2 * z + 1) * count])
        odd = fold_small(dw[(2 * z + 1) * count : (2 * z + 2) * count])
        keep_ref[z] = jnp.where(first, even, odd).astype(BF16)
        send_ref[z] = jnp.where(first, odd, even).astype(BF16)


def plus(a, b):
    return (a.astype(F32) + b.astype(F32)).astype(BF16)


def fold_core_kernel(wide, wide_in, deep, deep_in, stat, stat_in, wide_keep, wide_send, deep_keep, deep_send, stat_out):
    for y in range(2):
        wide_keep[y] = plus(wide[y, 0], wide_in[y, 0])
        wide_send[y] = plus(wide[y, 1], wide_in[y, 1])
    for x in range(2):
        deep_keep[x] = plus(deep[0, x], deep_in[0, x])
        deep_send[x] = plus(deep[1, x], deep_in[1, x])
    stat_out[...] = stat[...] + stat_in[...]


def fold_link_kernel(wide, wide_in, deep, deep_in, stat, stat_in, wide_keep, wide_send, deep_keep, deep_send, stat_out):
    wide_keep[...] = plus(wide[0], wide_in[0])
    wide_send[...] = plus(wide[1], wide_in[1])
    deep_keep[...] = plus(deep[0], deep_in[0])
    deep_send[...] = plus(deep[1], deep_in[1])
    stat_out[...] = stat[...] + stat_in[...]


def fold_far_kernel(wide, wide_in, deep, deep_in, small, small_in, stat, stat_in, block_ref):
    stats = stat[...] + stat_in[...]
    high = stats.astype(BF16)
    stats = jnp.concatenate([high.astype(F32), stats - high.astype(F32)], axis=0)
    stats = fold_lanes(stats).astype(BF16)
    edge = 0
    for ours, theirs in ((wide, wide_in), (deep, deep_in), (small, small_in)):
        count = ours.shape[1]
        block_ref[:, edge : edge + count] = plus(ours[...], theirs[...])
        edge += count
    for z in range(block_ref.shape[0]):
        block_ref[z, edge:] = stats


def finish_kernel(block_ref, d_qkv, d_out, d_in, d_down, gains_ref, biases_ref, rms_ref, total):
    acc = block_ref[0].astype(F32)
    for z in range(1, block_ref.shape[0]):
        acc = acc + block_ref[z].astype(F32)
    total[...] = acc
    width, wide_rows = d_out.shape
    d_out[...] = total[0:wide_rows, :width].T
    d_in[...] = total[0:wide_rows, width:].T
    edge = wide_rows + 2 * d_down.shape[0]
    d_down[...] = unfold_lanes(total[wide_rows:edge])
    count = d_qkv.shape[0]
    top = small_rows(count)
    small = total[edge : edge + top]
    d_qkv[...] = jnp.concatenate([small[:, :width], small[: count - top, width:]], axis=0)
    stats = unfold_lanes(total[edge + top :])
    stats = stats[:8] + stats[8:]
    gains_ref[...] = stats[0:2]
    biases_ref[...] = stats[2:4]
    count = jnp.max(stats[7:8], axis=1, keepdims=True)
    square = jnp.sum(stats[4:7], axis=1, keepdims=True)
    means = jnp.sqrt(square / (count * stats.shape[1]))
    here = lax.broadcasted_iota(jnp.int32, (3, 3), 0) == lax.broadcasted_iota(jnp.int32, (3, 3), 1)
    rms_ref[...] = jnp.sum(jnp.where(here, jnp.broadcast_to(means, (3, 3)), 0.0), axis=0, keepdims=True)


def mean_of(value):
    return jnp.mean(value, axis=-1, keepdims=True)


def col_sum(value):
    return jnp.sum(value, axis=0, keepdims=True)


def gelu_pair(pre):
    upper = 0.5 * (1.0 + lax.erf(pre * RSQRT2))
    slope = upper + pre * (jnp.exp(-0.5 * pre * pre) * RSQRT2PI)
    return pre * upper, slope


def middle_kernel(len_ref, place_ref, *rest, groups, sequences):
    ctx_refs, rest = rest[: groups * sequences], rest[groups * sequences :]
    tok_ref, cot_ref, gain_ref, bias_ref, rest = *rest[:4], rest[4:]
    wides, deeps, rest = rest[:8], rest[8:16], rest[16:]
    out_ref, mix_ref, rest = rest[0], rest[1], rest[2:]
    sends, rest = rest[: groups * sequences], rest[groups * sequences :]
    keep_w, send_w, keep_d, send_d, stats, w_out, w_in, w_down, hid, slope, acc_a, acc_d, held = rest
    place = place_ref[0]
    first = place_ref[1] == 0
    rows = tok_ref.shape[1]
    model = tok_ref.shape[2]
    width = model // groups
    shards = 2 * wides[0].shape[0]
    wide_rows, deep_rows = model // shards, width // shards

    for core in range(2):
        for y in range(2):
            g = place ^ (2 * y + core)

            def lay_wide(f, block):
                w_out[g, f * wide_rows : (f + 1) * wide_rows] = block[:, :width]
                w_in[g, f * wide_rows : (f + 1) * wide_rows] = block[:, width:]

            def lay_deep(f, block):
                w_down[g, f * deep_rows : (f + 1) * deep_rows] = unfold_lanes(block)

            lay_pairs(wides[core * 4 + y * 2], wides[core * 4 + y * 2 + 1], first, lay_wide)
            lay_pairs(deeps[core * 4 + y * 2], deeps[core * 4 + y * 2 + 1], first, lay_deep)
    for n in range(sequences):
        for s in range(groups):
            held[n, s] = ctx_refs[n * groups + s][...]
    acc_a[...] = jnp.zeros_like(acc_a)
    acc_d[...] = jnp.zeros_like(acc_d)
    stats[...] = jnp.zeros_like(stats)
    gain0, gain1 = gain_ref[0:1, :], gain_ref[1:2, :]
    bias0, bias1 = bias_ref[0:1, :], bias_ref[1:2, :]

    @pl.loop(0, sequences)
    def _(n):
        spot = lax.broadcasted_iota(jnp.int32, (rows, 1), 0) + place * rows
        valid = (spot < len_ref[n]).astype(F32)
        tokens = tok_ref[n].astype(F32)
        contexts = [unpack(held[n, s]) for s in range(groups)]
        attention = dot_nt(contexts[0], w_out[place])
        for s in range(1, groups):
            attention = attention + dot_nt(contexts[s], w_out[place ^ s])
        mixed = tokens + attention
        centered = mixed - mean_of(mixed)
        inv0 = lax.rsqrt(mean_of(centered * centered) + EPS)
        xhat0 = centered * inv0
        first = xhat0 * gain0 + bias0
        ffn_in = first.astype(BF16)
        pieces = []
        for g in range(groups):
            cols = slice(g * width, (g + 1) * width)
            pre = dot_nt(ffn_in[:, cols], w_in[g])
            hidden, tilt = gelu_pair(pre)
            hidden = hidden.astype(BF16)
            hid[g] = hidden
            slope[g] = tilt
            pieces.append(dot_nt(hidden, w_down[g]))
        ffn = jnp.concatenate(pieces, axis=1).astype(BF16).astype(F32)
        second = first + ffn
        centered = second - mean_of(second)
        inv1 = lax.rsqrt(mean_of(centered * centered) + EPS)
        xhat1 = centered * inv1
        out_ref[n] = ((xhat1 * gain1 + bias1) * valid).astype(BF16)
        upstream = cot_ref[n].astype(F32) * valid
        scaled = upstream * gain1
        g_second = inv1 * (scaled - mean_of(scaled) - xhat1 * mean_of(scaled * xhat1))
        g_ffn = g_second.astype(BF16)
        pieces = []
        for g in range(groups):
            cols = slice(g * width, (g + 1) * width)
            g_hidden = dot_nn(g_ffn[:, cols], w_down[g]).astype(BF16).astype(F32)
            g_pre = (g_hidden * slope[g]).astype(BF16)
            acc_d[g] += dot_tn(g_ffn[:, cols], hid[g])
            acc_a[1, g] += dot_tn(g_pre, ffn_in[:, cols])
            pieces.append(dot_nn(g_pre, w_in[g]))
        g_input = jnp.concatenate(pieces, axis=1).astype(BF16).astype(F32)
        upper = g_second + g_input
        scaled = upper * gain0
        g_mix = inv0 * (scaled - mean_of(scaled) - xhat0 * mean_of(scaled * xhat0))
        mix_ref[n] = g_mix
        g_attn = g_mix.astype(BF16)
        for s in range(groups):
            acc_a[0, place ^ s] += dot_tn(g_attn, contexts[s])
            held[n, s] = pack(dot_nn(g_attn, w_out[place ^ s]).astype(BF16))
        stats[0:1] += col_sum(upper * xhat0)
        stats[1:2] += col_sum(upstream * xhat1)
        stats[2:3] += col_sum(upper)
        stats[3:4] += col_sum(upstream)
        stats[4:5] += col_sum(tokens * tokens * valid)
        stats[5:6] += col_sum(attention * attention * valid)
        stats[6:7] += col_sum(ffn * ffn * valid)
        stats[7:8] += jnp.broadcast_to(jnp.sum(valid, axis=0, keepdims=True), (1, model))

    for n in range(sequences):
        for s in range(groups):
            sends[n * groups + s][...] = held[n, s]
    for core, (wide, deep) in enumerate(((keep_w, keep_d), (send_w, send_d))):
        for y in range(2):
            g = place ^ (2 * y + core)
            for z in range(shards // 2):
                blocks = []
                for f in (2 * z, 2 * z + 1):
                    at = slice(f * wide_rows, (f + 1) * wide_rows)
                    down = acc_d[g, f * deep_rows : (f + 1) * deep_rows]
                    blocks.append((jnp.concatenate([acc_a[0, g, at], acc_a[1, g, at]], axis=1), fold_lanes(down)))
                for x in range(2):
                    wide[y, x, z] = jnp.where(first, blocks[x][0], blocks[1 - x][0]).astype(BF16)
                    deep[y, x, z] = jnp.where(first, blocks[x][1], blocks[1 - x][1]).astype(BF16)


def flip(value, axis, bit):
    size = lax.axis_size(axis)
    return lax.ppermute(value, axis, [(i, i ^ bit) for i in range(size)])


def tp_exchange(chunks):
    order = sorted(range(1, len(chunks)), reverse=True)
    moved = {s: flip(chunks[s], "tp", s) for s in order}
    return [chunks[0]] + [moved[s] for s in range(1, len(chunks))]


def far_exchange(value):
    groups = [list(range(bit, lax.axis_size("fsdp"), 2)) for bit in range(2)]
    return lax.all_to_all(value, "fsdp", 0, 0, axis_index_groups=groups)


def on_device(tokens, cotangent, lengths, qkv_weight, out_weight, in_weight, down_weight, gains, biases):
    groups = lax.axis_size("tp")
    shards = lax.axis_size("fsdp")
    place = jnp.stack([lax.axis_index("tp"), lax.axis_index("fsdp") % 2]).astype(jnp.int32)
    rows, sequences, model = tokens.shape
    width = model // groups
    hidden = in_weight.shape[1] * shards
    positions = rows * groups
    packed = rows * 3 // 2
    far = shards // 2
    wide_rows, deep_rows, small = model // shards, 2 * width // shards, small_rows(3 * width // shards)
    vmem = pl.BlockSpec(memory_space=pltpu.VMEM)
    smem = pl.BlockSpec(memory_space=pltpu.SMEM)

    def shape(dims, kind=BF16):
        return jax.ShapeDtypeStruct(dims, kind)

    def call(kernel, outs, *operands, scalars=0, scratch=()):
        return pl.pallas_call(
            kernel,
            out_shape=outs,
            in_specs=[smem] * scalars + [vmem] * (len(operands) - scalars),
            out_specs=jax.tree.map(lambda _: vmem, outs),
            scratch_shapes=list(scratch),
        )(*operands)

    one = shape((packed, LANES))
    both = shape((sequences, packed, LANES))
    by_sequence = shape((sequences, rows, model))

    edge = wide_rows + deep_rows
    qkv_block = qkv_weight.T
    sent = call(
        prepare_kernel,
        shape((far, edge + small, 2 * width)),
        qkv_block,
        out_weight,
        in_weight,
        down_weight.T,
    )
    near = far_exchange(sent)
    tok_rows, *grouped = call(
        split_kernel,
        (by_sequence,) + (both,) * groups,
        place,
        tokens,
        scalars=1,
        scratch=[pltpu.VMEM((groups, sequences, packed, LANES), BF16)],
    )
    grouped = tp_exchange(grouped)
    cot_rows = call(part_kernel, by_sequence, cotangent)
    wide, deep, qkv = near[:, :wide_rows], near[:, wide_rows:edge], near[:, edge:]
    qkv = [qkv, flip(qkv, "fsdp", 1)]
    wide_y = flip(wide, "tp", 2)
    deep_x = flip(deep, "fsdp", 1)
    wides = [wide, flip(wide, "fsdp", 1), wide_y, flip(wide_y, "fsdp", 1)]
    deeps = [deep, deep_x, flip(deep, "tp", 2), flip(deep_x, "tp", 2)]
    wides += [flip(value, "tp", 1) for value in wides]
    deeps += [flip(value, "tp", 1) for value in deeps]

    heads = width // HD
    lse, context, mine = [], [], []
    for n in range(sequences):
        *chunks, sums = call(
            partial(attend_kernel, block=rows, parts=groups, n=n),
            (one,) * groups + (shape((heads, groups, 1, rows), F32),),
            lengths,
            place,
            *grouped,
            *qkv,
            scalars=2,
            scratch=[
                pltpu.VMEM((3 * width, width), BF16),
                pltpu.VMEM((positions, width), BF16),
                pltpu.VMEM((3 * heads, positions, HD), BF16),
                pltpu.VMEM((heads, positions, HD), BF16),
                pltpu.VMEM((groups, packed, LANES), BF16),
            ],
        )
        lse.append(sums)
        context.append(chunks)
        mine += tp_exchange(chunks)

    half_w = shape((2, 2, far, wide_rows, 2 * width))
    half_d = shape((2, 2, far, deep_rows, 2 * width))
    out_rows, g_mix, *rest = call(
        partial(middle_kernel, groups=groups, sequences=sequences),
        (by_sequence, shape((sequences, rows, model), F32))
        + (one,) * (groups * sequences)
        + (half_w, half_w, half_d, half_d, shape((8, model), F32)),
        lengths,
        place,
        *mine,
        tok_rows,
        cot_rows,
        gains,
        biases,
        *wides,
        *deeps,
        scalars=2,
        scratch=[
            pltpu.VMEM((groups, model, width), BF16),
            pltpu.VMEM((groups, hidden, width), BF16),
            pltpu.VMEM((groups, width, hidden), BF16),
            pltpu.VMEM((groups, rows, hidden), BF16),
            pltpu.VMEM((groups, rows, hidden), F32),
            pltpu.VMEM((2, groups, model, width), F32),
            pltpu.VMEM((groups, width, hidden), F32),
            pltpu.VMEM((sequences, groups, packed, LANES), BF16),
        ],
    )
    upstream = [tp_exchange(rest[n * groups : (n + 1) * groups]) for n in range(sequences)]
    keep_w, send_w, keep_d, send_d, stats = rest[groups * sequences :]
    output = call(merge_kernel, shape(tokens.shape), out_rows)

    pair_w, pair_d = shape(half_w.shape[1:]), shape(half_d.shape[1:])
    part_w, part_d = shape(half_w.shape[2:]), shape(half_d.shape[2:])
    sums = shape(stats.shape, F32)
    keep_w, send_w, keep_d, send_d, stats = call(
        fold_core_kernel,
        (pair_w, pair_w, pair_d, pair_d, sums),
        keep_w,
        flip(send_w, "tp", 1),
        keep_d,
        flip(send_d, "tp", 1),
        stats,
        flip(stats, "tp", 1),
    )
    keep_w, send_w, keep_d, send_d, stats = call(
        fold_link_kernel,
        (part_w, part_w, part_d, part_d, sums),
        keep_w,
        flip(send_w, "fsdp", 1),
        keep_d,
        flip(send_d, "tp", 2),
        stats,
        flip(stats, "fsdp", 1),
    )
    wide_in = flip(send_w, "tp", 2)
    deep_in = flip(send_d, "fsdp", 1)
    stats_in = flip(stats, "tp", 2)

    back, d_qkv = [], []
    for n in range(sequences):
        last = n == sequences - 1
        quarter = shape((far, small, 2 * width))
        full = shape((3 * width, width), F32)
        scratch = [
            pltpu.VMEM((3 * width, width), BF16),
            pltpu.VMEM((positions, width), BF16),
            pltpu.VMEM((3 * heads, positions, HD), BF16),
            pltpu.VMEM((3 * heads, positions, HD), BF16),
            pltpu.VMEM((heads, positions, HD), BF16),
            pltpu.VMEM((heads, groups, 1, rows), F32),
            pltpu.VMEM((groups, packed, LANES), BF16),
        ]
        outs = (one,) * groups + ((quarter, quarter) if last else (full,))
        if last:
            scratch.insert(0, pltpu.VMEM((3 * width, width), F32))
        *chunks, = call(
            partial(attend_back_kernel, block=rows, parts=groups, n=n, last_call=last),
            outs,
            lengths,
            place,
            *grouped,
            *upstream[n],
            *context[n],
            *qkv,
            lse[n],
            *d_qkv,
            scalars=2,
            scratch=scratch,
        )
        d_qkv = chunks[groups:]
        back += tp_exchange(chunks[:groups])
    keep_q, send_q = d_qkv

    blocks = call(
        fold_far_kernel,
        shape((far, edge + small + 32, 2 * width)),
        keep_w,
        wide_in,
        keep_d,
        deep_in,
        keep_q,
        flip(send_q, "fsdp", 1),
        stats,
        stats_in,
    )
    blocks = far_exchange(blocks)
    d_input = call(
        join_kernel,
        shape(tokens.shape, F32),
        place,
        g_mix,
        *back,
        scalars=1,
        scratch=[pltpu.VMEM((groups, sequences, packed, LANES), BF16)],
    )
    d_qkv, d_out, d_in, d_down, d_gains, d_biases, rms = call(
        finish_kernel,
        (
            shape(qkv_block.shape, F32),
            shape(out_weight.shape, F32),
            shape(in_weight.shape, F32),
            shape(down_weight.shape[::-1], F32),
            shape(gains.shape, F32),
            shape(biases.shape, F32),
            shape((1, 3), F32),
        ),
        blocks,
        scratch=[pltpu.VMEM(blocks.shape[1:], F32)],
    )
    return output, d_input, d_qkv.T, d_out, d_in, d_down.T, d_gains, d_biases, rms[0]


def solution(mesh):
    in_specs = (
        P("tp", "fsdp", None),
        P("tp", "fsdp", None),
        P("fsdp"),
        P("tp", "fsdp"),
        P("tp", "fsdp"),
        P("tp", "fsdp"),
        P("tp", "fsdp"),
        P(),
        P(),
    )
    out_specs = (
        P("tp", "fsdp", None),
        P("tp", "fsdp", None),
        P("tp", "fsdp"),
        P("tp", "fsdp"),
        P("tp", "fsdp"),
        P("tp", "fsdp"),
        P(),
        P(),
        P(),
    )
    return jax.shard_map(
        on_device, mesh=mesh, in_specs=in_specs, out_specs=out_specs, check_vma=False
    )
```

```python
from functools import partial

import jax
import jax.numpy as jnp
from jax import lax
from jax.experimental import pallas as pl
from jax.experimental.pallas import tpu as pltpu
from jax.sharding import PartitionSpec as P


HD = 64
LANES = 128
SCALE = 0.125
EPS = 1e-12
NEG = -1e30
RSQRT2 = 0.7071067811865476
RSQRT2PI = 0.3989422804014327
F32 = jnp.float32
BF16 = jnp.bfloat16


def dot_nn(a, b):
    return lax.dot_general(a, b, (((1,), (0,)), ((), ())), preferred_element_type=F32)


def dot_nt(a, b):
    return lax.dot_general(a, b, (((1,), (1,)), ((), ())), preferred_element_type=F32)


def dot_tn(a, b):
    return lax.dot_general(a, b, (((0,), (0,)), ((), ())), preferred_element_type=F32)


def pack(value):
    half = value.shape[0] // 2
    tail = value[:, LANES:]
    return jnp.concatenate(
        [value[:, :LANES], jnp.concatenate([tail[:half], tail[half:]], axis=1)], axis=0
    )


def unpack(block):
    rows = block.shape[0] * 2 // 3
    tail = block[rows:]
    return jnp.concatenate(
        [block[:rows], jnp.concatenate([tail[:, :HD], tail[:, HD:]], axis=0)], axis=1
    )


def lay_pairs(near, other, first, emit):
    for z in range(near.shape[0]):
        own, far = near[z], other[z]
        emit(2 * z, jnp.where(first, own, far))
        emit(2 * z + 1, jnp.where(first, far, own))


def fold_lanes(value):
    half = value.shape[1] // 2
    return jnp.concatenate([value[:, :half], value[:, half:]], axis=0)


def unfold_lanes(value):
    half = value.shape[0] // 2
    return jnp.concatenate([value[:half], value[half:]], axis=1)


def small_rows(count):
    return (count // 2 + 7) // 8 * 8


def fold_small(value):
    top = small_rows(value.shape[0])
    lower = value[top:]
    fill = jnp.zeros((2 * top - value.shape[0], value.shape[1]), value.dtype)
    return jnp.concatenate([value[:top], jnp.concatenate([lower, fill], axis=0)], axis=1)


def prepare_kernel(qkv_ref, out_ref, in_ref, down_ref, block_ref):
    wide = jnp.concatenate([out_ref[...].astype(F32).T, in_ref[...].astype(F32).T], axis=1)
    deep = fold_lanes(down_ref[...].astype(F32))
    small = fold_small(qkv_ref[...].astype(F32))
    block = jnp.concatenate([wide, deep, small], axis=0).astype(BF16)
    for z in range(block_ref.shape[0]):
        block_ref[z] = block


def split_kernel(place_ref, tok_ref, tok_out, *rest):
    sends, held = rest[:-1], rest[-1]
    groups = len(sends)
    width = tok_ref.shape[2] // groups
    for n in range(tok_ref.shape[1]):
        rows = tok_ref[:, n, :]
        tok_out[n] = rows
        for g in range(groups):
            held[g, n] = pack(rows[:, g * width : (g + 1) * width])
    for s in range(groups):
        sends[s][...] = held[place_ref[0] ^ s]


def part_kernel(in_ref, out_ref):
    for n in range(in_ref.shape[1]):
        out_ref[n] = in_ref[:, n, :]


def merge_kernel(in_ref, out_ref):
    for n in range(in_ref.shape[0]):
        out_ref[:, n, :] = in_ref[n]


def join_kernel(place_ref, mix_ref, *rest):
    backs, out_ref, held = rest[:-2], rest[-2], rest[-1]
    sequences = mix_ref.shape[0]
    groups = len(backs) // sequences
    for n in range(sequences):
        for s in range(groups):
            held[place_ref[0] ^ s, n] = backs[n * groups + s][...]
    for n in range(sequences):
        pulled = jnp.concatenate([unpack(held[g, n]) for g in range(groups)], axis=1)
        out_ref[:, n, :] = mix_ref[n] + pulled.astype(F32)


def load_heads(place_ref, chunk_refs, qkv_refs, tokens, weight, parts_ref, n, block):
    near_ref, other_ref = qkv_refs
    count = weight.shape[0] // (2 * near_ref.shape[0])
    top = small_rows(count)

    def lay_small(f, value):
        half = value.shape[1] // 2
        weight[f * count : f * count + top] = value[:, :half]
        weight[f * count + top : (f + 1) * count] = value[: count - top, half:]

    lay_pairs(near_ref, other_ref, place_ref[1] == 0, lay_small)
    for s in range(len(chunk_refs)):
        start = pl.multiple_of((place_ref[0] ^ s) * block, block)
        tokens[pl.ds(start, block)] = unpack(chunk_refs[s][n])
    projected = dot_nt(tokens[...], weight[...]).astype(BF16)
    for i in range(parts_ref.shape[0]):
        parts_ref[i] = projected[:, i * HD : (i + 1) * HD]


def masked_scores(keys, query, length):
    raw = dot_nt(keys, query)
    span, block = raw.shape
    edge = span - block
    spot = lax.broadcasted_iota(jnp.int32, (block, block), 0) + edge
    last = jnp.where(spot < length, raw[edge:], NEG)
    return jnp.concatenate([raw[:edge], last], axis=0) if edge else last


def for_span(length, block, parts, body):
    for count in range(1, parts + 1):
        span = count * block
        pl.when((length > span - block) & (length <= span))(partial(body, count, span))


def attend_kernel(len_ref, place_ref, *rest, block, parts, n):
    chunk_refs, qkv_refs, rest = rest[:parts], rest[parts : parts + 2], rest[parts + 2 :]
    sends, (lse_ref, weight, tokens, pieces, mixed, held) = rest[:parts], rest[parts:]
    length = len_ref[n]
    heads = pieces.shape[0] // 3
    load_heads(place_ref, chunk_refs, qkv_refs, tokens, weight, pieces, n, block)
    mixed[...] = jnp.zeros_like(mixed)
    lse_ref[...] = jnp.zeros_like(lse_ref)

    def body(count, span):
        @pl.loop(0, heads)
        def _(h):
            values_t = pieces[2 * heads + h, 0:span].T

            for b in range(count):
                at = slice(b * block, (b + 1) * block)
                query = (pieces[h, at] * SCALE).astype(BF16)
                masked = masked_scores(pieces[heads + h, 0:span], query, length)
                top = jnp.max(masked, axis=0, keepdims=True)
                terms = jnp.exp(masked - top)
                total = jnp.sum(terms, axis=0, keepdims=True)
                mixed[h, at] = (dot_nn(values_t, terms.astype(BF16)) / total).T.astype(BF16)
                lse_ref[h, b] = top + jnp.log(total)

    for_span(length, block, parts, body)
    for i in range(parts):
        rows = slice(i * block, (i + 1) * block)
        held[i] = pack(jnp.concatenate([mixed[h, rows] for h in range(heads)], axis=1))
    for s in range(parts):
        sends[s][...] = held[place_ref[0] ^ s]


def attend_back_kernel(len_ref, place_ref, *rest, block, parts, n, last_call):
    chunk_refs, g_refs, ctx_refs = rest[:parts], rest[parts : 2 * parts], rest[2 * parts : 3 * parts]
    qkv_refs, lse_ref, rest = rest[3 * parts : 3 * parts + 2], rest[3 * parts + 2], rest[3 * parts + 3 :]
    if last_call:
        start_ref, rest = rest[0], rest[1:]
    sends, rest = rest[:parts], rest[parts:]
    if last_call:
        keep_ref, send_ref, rest = rest[0], rest[1], rest[2:]
    dw, weight, tokens, pieces, dpieces, grad, delta, held = rest
    length = len_ref[n]
    heads = pieces.shape[0] // 3
    shards = 2 * qkv_refs[0].shape[0]
    load_heads(place_ref, chunk_refs, qkv_refs, tokens, weight, pieces, n, block)
    for s in range(parts):
        spot = place_ref[0] ^ s
        at = pl.ds(pl.multiple_of(spot * block, block), block)
        piece = unpack(g_refs[s][...])
        both_t = (piece.astype(F32) * unpack(ctx_refs[s][...]).astype(F32)).T
        for h in range(heads):
            grad[h, at] = piece[:, h * HD : (h + 1) * HD]
            delta[h, spot] = jnp.sum(both_t[h * HD : (h + 1) * HD], axis=0, keepdims=True)
    dpieces[...] = jnp.zeros_like(dpieces)

    def body(count, span):
        @pl.loop(0, heads)
        def _(h):
            keys_t = pieces[heads + h, 0:span].T
            sum_k = sum_v = jnp.zeros((span, HD), F32)
            for b in range(count):
                at = slice(b * block, (b + 1) * block)
                query = (pieces[h, at] * SCALE).astype(BF16)
                upstream = grad[h, at]
                probs = jnp.exp(masked_scores(pieces[heads + h, 0:span], query, length) - lse_ref[h, b])
                dprobs = dot_nt(pieces[2 * heads + h, 0:span], upstream)
                dscores = (probs * (dprobs - delta[h, b])).astype(BF16)
                sum_v = sum_v + dot_nn(probs.astype(BF16), upstream)
                sum_k = sum_k + dot_nn(dscores, query)
                dpieces[h, at] = (dot_nn(keys_t, dscores) * SCALE).T.astype(BF16)

            dpieces[heads + h, 0:span] = sum_k.astype(BF16)
            dpieces[2 * heads + h, 0:span] = sum_v.astype(BF16)

    for_span(length, block, parts, body)
    dprojected = jnp.concatenate([dpieces[i] for i in range(3 * heads)], axis=1)
    back = dot_nn(dprojected, weight[...]).astype(BF16)
    for i in range(parts):
        held[i] = pack(back[i * block : (i + 1) * block])
    for s in range(parts):
        sends[s][...] = held[place_ref[0] ^ s]
    total = dot_tn(dprojected, tokens[...])
    if not last_call:
        dw[...] = total
        return
    dw[...] = total + start_ref[...]
    count = dw.shape[0] // shards
    first = place_ref[1] == 0
    for z in range(shards // 2):
        even = fold_small(dw[2 * z * count : (2 * z + 1) * count])
        odd = fold_small(dw[(2 * z + 1) * count : (2 * z + 2) * count])
        keep_ref[z] = jnp.where(first, even, odd).astype(BF16)
        send_ref[z] = jnp.where(first, odd, even).astype(BF16)


def plus(a, b):
    return (a.astype(F32) + b.astype(F32)).astype(BF16)


def fold_core_kernel(wide, wide_in, deep, deep_in, stat, stat_in, wide_keep, wide_send, deep_keep, deep_send, stat_out):
    for y in range(2):
        wide_keep[y] = plus(wide[y, 0], wide_in[y, 0])
        wide_send[y] = plus(wide[y, 1], wide_in[y, 1])
    for x in range(2):
        deep_keep[x] = plus(deep[0, x], deep_in[0, x])
        deep_send[x] = plus(deep[1, x], deep_in[1, x])
    stat_out[...] = stat[...] + stat_in[...]


def fold_link_kernel(wide, wide_in, deep, deep_in, stat, stat_in, wide_keep, wide_send, deep_keep, deep_send, stat_out):
    wide_keep[...] = plus(wide[0], wide_in[0])
    wide_send[...] = plus(wide[1], wide_in[1])
    deep_keep[...] = plus(deep[0], deep_in[0])
    deep_send[...] = plus(deep[1], deep_in[1])
    stat_out[...] = stat[...] + stat_in[...]


def fold_far_kernel(wide, wide_in, deep, deep_in, small, small_in, stat, stat_in, block_ref):
    stats = stat[...] + stat_in[...]
    high = stats.astype(BF16)
    stats = jnp.concatenate([high.astype(F32), stats - high.astype(F32)], axis=0)
    stats = fold_lanes(stats).astype(BF16)
    edge = 0
    for ours, theirs in ((wide, wide_in), (deep, deep_in), (small, small_in)):
        count = ours.shape[1]
        block_ref[:, edge : edge + count] = plus(ours[...], theirs[...])
        edge += count
    for z in range(block_ref.shape[0]):
        block_ref[z, edge:] = stats


def finish_kernel(block_ref, d_qkv, d_out, d_in, d_down, gains_ref, biases_ref, rms_ref, total):
    acc = block_ref[0].astype(F32)
    for z in range(1, block_ref.shape[0]):
        acc = acc + block_ref[z].astype(F32)
    total[...] = acc
    width, wide_rows = d_out.shape
    d_out[...] = total[0:wide_rows, :width].T
    d_in[...] = total[0:wide_rows, width:].T
    edge = wide_rows + 2 * d_down.shape[0]
    d_down[...] = unfold_lanes(total[wide_rows:edge])
    count = d_qkv.shape[0]
    top = small_rows(count)
    small = total[edge : edge + top]
    d_qkv[...] = jnp.concatenate([small[:, :width], small[: count - top, width:]], axis=0)
    stats = unfold_lanes(total[edge + top :])
    stats = stats[:8] + stats[8:]
    gains_ref[...] = stats[0:2]
    biases_ref[...] = stats[2:4]
    count = jnp.max(stats[7:8], axis=1, keepdims=True)
    square = jnp.sum(stats[4:7], axis=1, keepdims=True)
    means = jnp.sqrt(square / (count * stats.shape[1]))
    here = lax.broadcasted_iota(jnp.int32, (3, 3), 0) == lax.broadcasted_iota(jnp.int32, (3, 3), 1)
    rms_ref[...] = jnp.sum(jnp.where(here, jnp.broadcast_to(means, (3, 3)), 0.0), axis=0, keepdims=True)


def mean_of(value):
    return jnp.mean(value, axis=-1, keepdims=True)


def col_sum(value):
    return jnp.sum(value, axis=0, keepdims=True)


def gelu_pair(pre):
    upper = 0.5 * (1.0 + lax.erf(pre * RSQRT2))
    slope = upper + pre * (jnp.exp(-0.5 * pre * pre) * RSQRT2PI)
    return pre * upper, slope


def middle_kernel(len_ref, place_ref, *rest, groups, sequences):
    ctx_refs, rest = rest[: groups * sequences], rest[groups * sequences :]
    tok_ref, cot_ref, gain_ref, bias_ref, rest = *rest[:4], rest[4:]
    wides, deeps, rest = rest[:8], rest[8:16], rest[16:]
    out_ref, mix_ref, rest = rest[0], rest[1], rest[2:]
    sends, rest = rest[: groups * sequences], rest[groups * sequences :]
    keep_w, send_w, keep_d, send_d, stats, w_out, w_in, w_down, hid, slope, acc_a, acc_d = rest
    place = place_ref[0]
    side = place_ref[1] == 0
    rows = tok_ref.shape[1]
    model = tok_ref.shape[2]
    width = model // groups
    shards = 2 * wides[0].shape[0]
    wide_rows, deep_rows = model // shards, width // shards

    for core in range(2):
        for y in range(2):
            g = place ^ (2 * y + core)

            def lay_wide(f, block):
                w_out[g, f * wide_rows : (f + 1) * wide_rows] = block[:, :width]
                w_in[g, f * wide_rows : (f + 1) * wide_rows] = block[:, width:]

            def lay_deep(f, block):
                w_down[g, f * deep_rows : (f + 1) * deep_rows] = unfold_lanes(block)

            lay_pairs(wides[core * 4 + y * 2], wides[core * 4 + y * 2 + 1], side, lay_wide)
            lay_pairs(deeps[core * 4 + y * 2], deeps[core * 4 + y * 2 + 1], side, lay_deep)
    gain0, gain1 = gain_ref[0:1, :], gain_ref[1:2, :]
    bias0, bias1 = bias_ref[0:1, :], bias_ref[1:2, :]

    spot = lax.broadcasted_iota(jnp.int32, (rows, 1), 0) + place * rows
    valid = jnp.concatenate([(spot < len_ref[n]).astype(F32) for n in range(sequences)], axis=0)
    tokens = tok_ref[...].reshape(sequences * rows, model).astype(F32)
    contexts = [
        jnp.concatenate([unpack(ctx_refs[n * groups + s][...]) for n in range(sequences)], axis=0)
        for s in range(groups)
    ]
    attention = dot_nt(contexts[0], w_out[place])
    for s in range(1, groups):
        attention = attention + dot_nt(contexts[s], w_out[place ^ s])
    mixed = tokens + attention
    centered = mixed - mean_of(mixed)
    inv0 = lax.rsqrt(mean_of(centered * centered) + EPS)
    xhat0 = centered * inv0
    first = xhat0 * gain0 + bias0
    ffn_in = first.astype(BF16)
    pieces = []
    for g in range(groups):
        cols = slice(g * width, (g + 1) * width)
        pre = dot_nt(ffn_in[:, cols], w_in[g])
        hidden, tilt = gelu_pair(pre)
        hidden = hidden.astype(BF16)
        hid[g] = hidden
        slope[g] = tilt
        pieces.append(dot_nt(hidden, w_down[g]))
    ffn = jnp.concatenate(pieces, axis=1).astype(BF16).astype(F32)
    second = first + ffn
    centered = second - mean_of(second)
    inv1 = lax.rsqrt(mean_of(centered * centered) + EPS)
    xhat1 = centered * inv1
    out_ref[...] = ((xhat1 * gain1 + bias1) * valid).astype(BF16).reshape(sequences, rows, model)
    upstream = cot_ref[...].reshape(sequences * rows, model).astype(F32) * valid
    scaled = upstream * gain1
    g_second = inv1 * (scaled - mean_of(scaled) - xhat1 * mean_of(scaled * xhat1))
    g_ffn = g_second.astype(BF16)
    pieces = []
    for g in range(groups):
        cols = slice(g * width, (g + 1) * width)
        g_hidden = dot_nn(g_ffn[:, cols], w_down[g]).astype(BF16).astype(F32)
        g_pre = (g_hidden * slope[g]).astype(BF16)
        acc_d[g] = dot_tn(g_ffn[:, cols], hid[g])
        acc_a[1, g] = dot_tn(g_pre, ffn_in[:, cols])
        pieces.append(dot_nn(g_pre, w_in[g]))
    g_input = jnp.concatenate(pieces, axis=1).astype(BF16).astype(F32)
    upper = g_second + g_input
    scaled = upper * gain0
    g_mix = inv0 * (scaled - mean_of(scaled) - xhat0 * mean_of(scaled * xhat0))
    mix_ref[...] = g_mix.reshape(sequences, rows, model)
    g_attn = g_mix.astype(BF16)
    for s in range(groups):
        acc_a[0, place ^ s] = dot_tn(g_attn, contexts[s])
        pulled = dot_nn(g_attn, w_out[place ^ s]).astype(BF16)
        for n in range(sequences):
            sends[n * groups + s][...] = pack(pulled[n * rows : (n + 1) * rows])
    stats[0:1] = col_sum(upper * xhat0)
    stats[1:2] = col_sum(upstream * xhat1)
    stats[2:3] = col_sum(upper)
    stats[3:4] = col_sum(upstream)
    stats[4:5] = col_sum(tokens * tokens * valid)
    stats[5:6] = col_sum(attention * attention * valid)
    stats[6:7] = col_sum(ffn * ffn * valid)
    stats[7:8] = jnp.broadcast_to(jnp.sum(valid, axis=0, keepdims=True), (1, model))

    for core, (wide, deep) in enumerate(((keep_w, keep_d), (send_w, send_d))):
        for y in range(2):
            g = place ^ (2 * y + core)
            for z in range(shards // 2):
                blocks = []
                for f in (2 * z, 2 * z + 1):
                    at = slice(f * wide_rows, (f + 1) * wide_rows)
                    down = acc_d[g, f * deep_rows : (f + 1) * deep_rows]
                    blocks.append((jnp.concatenate([acc_a[0, g, at], acc_a[1, g, at]], axis=1), fold_lanes(down)))
                for x in range(2):
                    wide[y, x, z] = jnp.where(side, blocks[x][0], blocks[1 - x][0]).astype(BF16)
                    deep[y, x, z] = jnp.where(side, blocks[x][1], blocks[1 - x][1]).astype(BF16)


def flip(value, axis, bit):
    size = lax.axis_size(axis)
    return lax.ppermute(value, axis, [(i, i ^ bit) for i in range(size)])


def tp_exchange(chunks):
    order = sorted(range(1, len(chunks)), reverse=True)
    moved = {s: flip(chunks[s], "tp", s) for s in order}
    return [chunks[0]] + [moved[s] for s in range(1, len(chunks))]


def far_exchange(value):
    groups = [list(range(bit, lax.axis_size("fsdp"), 2)) for bit in range(2)]
    return lax.all_to_all(value, "fsdp", 0, 0, axis_index_groups=groups)


def on_device(tokens, cotangent, lengths, qkv_weight, out_weight, in_weight, down_weight, gains, biases):
    groups = lax.axis_size("tp")
    shards = lax.axis_size("fsdp")
    place = jnp.stack([lax.axis_index("tp"), lax.axis_index("fsdp") % 2]).astype(jnp.int32)
    rows, sequences, model = tokens.shape
    width = model // groups
    hidden = in_weight.shape[1] * shards
    positions = rows * groups
    packed = rows * 3 // 2
    far = shards // 2
    wide_rows, deep_rows, small = model // shards, 2 * width // shards, small_rows(3 * width // shards)
    vmem = pl.BlockSpec(memory_space=pltpu.VMEM)
    smem = pl.BlockSpec(memory_space=pltpu.SMEM)

    def shape(dims, kind=BF16):
        return jax.ShapeDtypeStruct(dims, kind)

    def call(kernel, outs, *operands, scalars=0, scratch=(), room=16):
        return pl.pallas_call(
            kernel,
            out_shape=outs,
            in_specs=[smem] * scalars + [vmem] * (len(operands) - scalars),
            out_specs=jax.tree.map(lambda _: vmem, outs),
            scratch_shapes=list(scratch),
            compiler_params=pltpu.CompilerParams(vmem_limit_bytes=room << 20),
        )(*operands)

    one = shape((packed, LANES))
    both = shape((sequences, packed, LANES))
    by_sequence = shape((sequences, rows, model))

    edge = wide_rows + deep_rows
    qkv_block = qkv_weight.T
    sent = call(
        prepare_kernel,
        shape((far, edge + small, 2 * width)),
        qkv_block,
        out_weight,
        in_weight,
        down_weight.T,
        room=60,
    )
    near = far_exchange(sent)
    tok_rows, *grouped = call(
        split_kernel,
        (by_sequence,) + (both,) * groups,
        place,
        tokens,
        scalars=1,
        scratch=[pltpu.VMEM((groups, sequences, packed, LANES), BF16)],
    )
    grouped = tp_exchange(grouped)
    cot_rows = call(part_kernel, by_sequence, cotangent)
    wide, deep, qkv = near[:, :wide_rows], near[:, wide_rows:edge], near[:, edge:]
    qkv = [qkv, flip(qkv, "fsdp", 1)]
    wide_y = flip(wide, "tp", 2)
    deep_x = flip(deep, "fsdp", 1)
    wides = [wide, flip(wide, "fsdp", 1), wide_y, flip(wide_y, "fsdp", 1)]
    deeps = [deep, deep_x, flip(deep, "tp", 2), flip(deep_x, "tp", 2)]
    wides += [flip(value, "tp", 1) for value in wides]
    deeps += [flip(value, "tp", 1) for value in deeps]

    heads = width // HD
    lse, context, mine = [], [], []
    for n in range(sequences):
        *chunks, sums = call(
            partial(attend_kernel, block=rows, parts=groups, n=n),
            (one,) * groups + (shape((heads, groups, 1, rows), F32),),
            lengths,
            place,
            *grouped,
            *qkv,
            scalars=2,
            room=12,
            scratch=[
                pltpu.VMEM((3 * width, width), BF16),
                pltpu.VMEM((positions, width), BF16),
                pltpu.VMEM((3 * heads, positions, HD), BF16),
                pltpu.VMEM((heads, positions, HD), BF16),
                pltpu.VMEM((groups, packed, LANES), BF16),
            ],
        )
        lse.append(sums)
        context.append(chunks)
        mine += tp_exchange(chunks)

    half_w = shape((2, 2, far, wide_rows, 2 * width))
    half_d = shape((2, 2, far, deep_rows, 2 * width))
    out_rows, g_mix, *rest = call(
        partial(middle_kernel, groups=groups, sequences=sequences),
        (by_sequence, shape((sequences, rows, model), F32))
        + (one,) * (groups * sequences)
        + (half_w, half_w, half_d, half_d, shape((8, model), F32)),
        lengths,
        place,
        *mine,
        tok_rows,
        cot_rows,
        gains,
        biases,
        *wides,
        *deeps,
        scalars=2,
        room=50,
        scratch=[
            pltpu.VMEM((groups, model, width), BF16),
            pltpu.VMEM((groups, hidden, width), BF16),
            pltpu.VMEM((groups, width, hidden), BF16),
            pltpu.VMEM((groups, sequences * rows, hidden), BF16),
            pltpu.VMEM((groups, sequences * rows, hidden), F32),
            pltpu.VMEM((2, groups, model, width), F32),
            pltpu.VMEM((groups, width, hidden), F32),
        ],
    )
    upstream = [tp_exchange(rest[n * groups : (n + 1) * groups]) for n in range(sequences)]
    keep_w, send_w, keep_d, send_d, stats = rest[groups * sequences :]
    output = call(merge_kernel, shape(tokens.shape), out_rows)

    pair_w, pair_d = shape(half_w.shape[1:]), shape(half_d.shape[1:])
    part_w, part_d = shape(half_w.shape[2:]), shape(half_d.shape[2:])
    sums = shape(stats.shape, F32)
    keep_w, send_w, keep_d, send_d, stats = call(
        fold_core_kernel,
        (pair_w, pair_w, pair_d, pair_d, sums),
        keep_w,
        flip(send_w, "tp", 1),
        keep_d,
        flip(send_d, "tp", 1),
        stats,
        flip(stats, "tp", 1),
    )
    keep_w, send_w, keep_d, send_d, stats = call(
        fold_link_kernel,
        (part_w, part_w, part_d, part_d, sums),
        keep_w,
        flip(send_w, "fsdp", 1),
        keep_d,
        flip(send_d, "tp", 2),
        stats,
        flip(stats, "fsdp", 1),
    )
    wide_in = flip(send_w, "tp", 2)
    deep_in = flip(send_d, "fsdp", 1)
    stats_in = flip(stats, "tp", 2)

    back, d_qkv = [], []
    for n in range(sequences):
        last = n == sequences - 1
        quarter = shape((far, small, 2 * width))
        full = shape((3 * width, width), F32)
        scratch = [
            pltpu.VMEM((3 * width, width), BF16),
            pltpu.VMEM((positions, width), BF16),
            pltpu.VMEM((3 * heads, positions, HD), BF16),
            pltpu.VMEM((3 * heads, positions, HD), BF16),
            pltpu.VMEM((heads, positions, HD), BF16),
            pltpu.VMEM((heads, groups, 1, rows), F32),
            pltpu.VMEM((groups, packed, LANES), BF16),
        ]
        outs = (one,) * groups + ((quarter, quarter) if last else (full,))
        if last:
            scratch.insert(0, pltpu.VMEM((3 * width, width), F32))
        *chunks, = call(
            partial(attend_back_kernel, block=rows, parts=groups, n=n, last_call=last),
            outs,
            lengths,
            place,
            *grouped,
            *upstream[n],
            *context[n],
            *qkv,
            lse[n],
            *d_qkv,
            scalars=2,
            room=20,
            scratch=scratch,
        )
        d_qkv = chunks[groups:]
        back += tp_exchange(chunks[:groups])
    keep_q, send_q = d_qkv

    blocks = call(
        fold_far_kernel,
        shape((far, edge + small + 32, 2 * width)),
        keep_w,
        wide_in,
        keep_d,
        deep_in,
        keep_q,
        flip(send_q, "fsdp", 1),
        stats,
        stats_in,
    )
    blocks = far_exchange(blocks)
    d_input = call(
        join_kernel,
        shape(tokens.shape, F32),
        place,
        g_mix,
        *back,
        scalars=1,
        scratch=[pltpu.VMEM((groups, sequences, packed, LANES), BF16)],
    )
    d_qkv, d_out, d_in, d_down, d_gains, d_biases, rms = call(
        finish_kernel,
        (
            shape(qkv_block.shape, F32),
            shape(out_weight.shape, F32),
            shape(in_weight.shape, F32),
            shape(down_weight.shape[::-1], F32),
            shape(gains.shape, F32),
            shape(biases.shape, F32),
            shape((1, 3), F32),
        ),
        blocks,
        scratch=[pltpu.VMEM(blocks.shape[1:], F32)],
    )
    return output, d_input, d_qkv.T, d_out, d_in, d_down.T, d_gains, d_biases, rms[0]


def solution(mesh):
    in_specs = (
        P("tp", "fsdp", None),
        P("tp", "fsdp", None),
        P("fsdp"),
        P("tp", "fsdp"),
        P("tp", "fsdp"),
        P("tp", "fsdp"),
        P("tp", "fsdp"),
        P(),
        P(),
    )
    out_specs = (
        P("tp", "fsdp", None),
        P("tp", "fsdp", None),
        P("tp", "fsdp"),
        P("tp", "fsdp"),
        P("tp", "fsdp"),
        P("tp", "fsdp"),
        P(),
        P(),
        P(),
    )
    return jax.shard_map(
        on_device, mesh=mesh, in_specs=in_specs, out_specs=out_specs, check_vma=False
    )
```
